256 devices in a mesh: dp: 16 (over y_hi, x, core), tensor: 16 (over z, y_lo).
Axes of the slice: x: 4, y: 4 (y_hi: 2, y_lo: 2; y = y_hi * 2 + y_lo), z: 8, core: 2. Of those that a mesh axis runs over, the one named last changes fastest.
Arguments:
- tokens: bfloat16 [8192, 8192], P('dp', 'tensor'), may hold values from -13 to 13
- proj: bfloat16 [8192, 8192], P('tensor'), may hold values from -8 to 8
- gain: float32 [8192], P('tensor'), may hold values from 0.1 to 1.9
- target: bfloat16 [8192, 8192], P('dp', 'tensor'), may hold values from -6 to 6
- adapter_down_weight: bfloat16 [256, 64, 8192], P('dp', None, 'tensor'), may hold values from -0.0625 to 0.0625
- adapter_up_weight: bfloat16 [256, 64, 8192], P('dp', None, 'tensor'), may hold values from -0.75 to 0.75
- source_row_index: int32 [16, 16, 96], P('dp'), may hold values from 0 to 512, as said below
- padded_row_index: int32 [16, 3584], P('dp'), may hold values from 0 to 1536, as said below
- padded_block_tenant: int32 [16, 28], P('dp'), may hold values from 0 to 15, as said below
Outputs:
- draft: bfloat16 [8192, 8192], P('dp', 'tensor')
- grad_down: bfloat16 [256, 64, 8192], P('dp', None, 'tensor')
- grad_up: bfloat16 [256, 64, 8192], P('dp', None, 'tensor')
The draws below stay inside these ranges and needn't reach their ends.
Inputs may be any that keep to these rules, and one draw needn't show every extreme that they name: For source s and owner d, the first c[s, d] entries of source_row_index[s, d] are rows of source s and the rest are 512; every row of a source appears exactly once over all owners. Some source fills all 96 slots to some owner, and some owner receives 96 rows from every source. `padded_row_index`: for owner d, every live slot s * 96 + j (source_row_index[s, d, j] < 512) appears exactly once, all other entries are 1536; the rows of one block of 128 padded rows belong to one tenant. `padded_block_tenant`: nondecreasing along the blocks of an owner.
All inputs are finite; a program needn't handle non-finite values.
Results may differ from the reference program's by a relative error of at most 0.02.
Values may be sent and summed in bfloat16 or wider, within the bound.
A program may use at most 128 MiB of HBM per device.

```python
import jax
import jax.numpy as jnp
from jax import lax

MODEL_WIDTH = 8192
ADAPTER_RANK = 64
TEN_DEV = 16
TOK_DEV = 512
BLOCK = 128
TOKENS = 8192
TENANT_COUNT = 256
CAP = 96
SLOTS = 1536
NBLK = 28
PAD = 3584
N_DP = 16
N_TENSOR = 16


def shuffle_rows(subkey):
    return jax.random.permutation(subkey, TOK_DEV)


def shuffle_tenants(subkey):
    return jax.random.permutation(subkey, TEN_DEV)


def owner_layout(is_live, tenants):
    slot_ids = jnp.arange(SLOTS, dtype=jnp.int32)
    sort_key = jnp.where(is_live, tenants * SLOTS + slot_ids, TEN_DEV * SLOTS + slot_ids)
    ordering = jnp.argsort(sort_key).astype(jnp.int32)
    member = ((tenants[:, None] == jnp.arange(TEN_DEV, dtype=jnp.int32)[None, :]) & is_live[:, None]).astype(jnp.int32)
    sizes = jnp.sum(member, axis=0)
    padded = (sizes + BLOCK - 1) // BLOCK * BLOCK
    pad_first = jnp.cumsum(padded) - padded
    row_first = jnp.cumsum(sizes) - sizes
    sorted_tenant = tenants[ordering]
    sorted_live = is_live[ordering]
    where_to = jnp.where(sorted_live, pad_first[sorted_tenant] + slot_ids - row_first[sorted_tenant], PAD)
    padded_row_index = jnp.full((PAD,), SLOTS, jnp.int32).at[where_to].set(ordering, mode='drop')
    block_starts = jnp.arange(NBLK, dtype=jnp.int32) * BLOCK
    padded_block_tenant = jnp.sum(((pad_first + padded)[None, :] <= block_starts[:, None]).astype(jnp.int32), axis=1)
    padded_block_tenant = jnp.minimum(padded_block_tenant, TEN_DEV - 1).astype(jnp.int32)
    return (padded_row_index, padded_block_tenant)


def routing_layout(key):
    subkeys = jax.random.split(jax.random.fold_in(key, 4099), 6)
    hot_count = N_DP // 4
    cold_count = N_DP - hot_count
    extra_rows = TOK_DEV // 4 - cold_count
    base_rank = jax.random.permutation(subkeys[0], N_DP)
    shifts = jax.random.randint(subkeys[1], (N_DP,), 0, 2)
    ranking = (base_rank[None, :] + shifts[:, None]) % N_DP
    offsets = jax.random.randint(subkeys[2], (N_DP, extra_rows), 0, 3)
    entries = (jnp.arange(extra_rows)[None, :] + offsets) % cold_count
    cold_sizes = 1 + jnp.sum((entries[:, :, None] == jnp.arange(cold_count)[None, None, :]).astype(jnp.int32), axis=1)
    cold_pick = jnp.take_along_axis(cold_sizes, jnp.clip(ranking - hot_count, 0, cold_count - 1), axis=1)
    counts = jnp.where(ranking < hot_count, CAP, cold_pick)
    firsts = jnp.cumsum(counts, axis=1) - counts
    row_perms = jax.vmap(shuffle_rows)(jax.random.split(subkeys[3], N_DP))
    slot_ids = jnp.arange(CAP)
    wanted = jnp.clip(firsts[:, :, None] + slot_ids[None, None, :], 0, TOK_DEV - 1)
    picked = row_perms[jnp.arange(N_DP)[:, None, None], wanted]
    is_live = slot_ids[None, None, :] < counts[:, :, None]
    source_row_index = jnp.where(is_live, picked, TOK_DEV).astype(jnp.int32)
    live_owner = jnp.transpose(is_live, (1, 0, 2)).reshape(N_DP, SLOTS)
    choose = jnp.min(jax.random.randint(subkeys[4], (N_DP, 2, SLOTS), 0, TEN_DEV), axis=1)
    tenant_perms = jax.vmap(shuffle_tenants)(jax.random.split(subkeys[5], N_DP))
    tenants = jnp.take_along_axis(tenant_perms, choose, axis=1).astype(jnp.int32)
    padded_row_index, padded_block_tenant = jax.vmap(owner_layout)(live_owner, tenants)
    return (source_row_index, padded_row_index, padded_block_tenant)


def draw_source_row_index(key, part):
    return routing_layout(key)[0]


def draw_padded_row_index(key, part):
    return routing_layout(key)[1]


def draw_padded_block_tenant(key, part):
    return routing_layout(key)[2]


def draw_tokens(key, part):
    subkeys = jax.random.split(jax.random.fold_in(key, 311), 2)
    row_scale = 10.0 ** jax.random.uniform(subkeys[0], (TOKENS, 1), minval=-0.5, maxval=0.5)
    entries = jax.random.truncated_normal(subkeys[1], -4.0, 4.0, (TOKENS, MODEL_WIDTH))
    return (row_scale * entries).astype(jnp.bfloat16)


def draw_proj(key, part):
    subkeys = jax.random.split(jax.random.fold_in(key, 577), 2)
    column_scale = 10.0 ** (jnp.arange(MODEL_WIDTH, dtype=jnp.float32) / MODEL_WIDTH) * jax.random.uniform(subkeys[0], (MODEL_WIDTH,), minval=0.7, maxval=1.3)
    entries = jax.random.truncated_normal(subkeys[1], -4.0, 4.0, (MODEL_WIDTH, MODEL_WIDTH))
    return (entries * column_scale[None, :] * MODEL_WIDTH ** (-0.5)).astype(jnp.bfloat16)


def shard_levels(stream_key, dims, cuts, low, top_value):
    def one(position, parts):
        draws = jax.random.uniform(jax.random.fold_in(jax.random.fold_in(stream_key, 6), position), (parts,), jnp.float32, low / len(cuts), top_value / len(cuts))
        return jnp.repeat(jnp.exp(draws), dims[position] // parts).reshape((-1,) + (1,) * (len(dims) - position - 1))

    level = one(*cuts[0])
    for cut in cuts[1:]:
        level = level * one(*cut)
    return level


def centred(own_key, shape, width, bound, cuts=(), kind=jnp.bfloat16):
    result = width * jax.random.normal(own_key, shape, jnp.float32)
    if cuts:
        result = result * shard_levels(own_key, shape, cuts, -0.22, 0.18)
    return jnp.clip(result, -bound, bound).astype(kind)


def setup_inputs(seed: int = 0) -> dict:
    key_of = jax.random.split(jax.random.key(seed), 10)
    tokens = draw_tokens(jax.random.fold_in(key_of[9], 71), 0)
    proj = draw_proj(jax.random.fold_in(key_of[9], 71), 0)
    gain = jnp.clip(1.0 + 0.18 * jax.random.normal(key_of[2], (MODEL_WIDTH,), jnp.float32), 0.1, 1.9)
    target = centred(key_of[3], (TOKENS, MODEL_WIDTH), 1.0, 6.0, ((0, 16), (1, 16)))
    adapter_down_weight = centred(key_of[4], (TENANT_COUNT, ADAPTER_RANK, MODEL_WIDTH), MODEL_WIDTH ** -0.5, 0.0625, ((0, 16), (2, 16)))
    adapter_up_weight = centred(key_of[5], (TENANT_COUNT, ADAPTER_RANK, MODEL_WIDTH), ADAPTER_RANK ** -0.5, 0.75, ((0, 16), (2, 16)))
    source_row_index = draw_source_row_index(jax.random.fold_in(key_of[9], 71), 0)
    padded_row_index = draw_padded_row_index(jax.random.fold_in(key_of[9], 71), 0)
    padded_block_tenant = draw_padded_block_tenant(jax.random.fold_in(key_of[9], 71), 0)
    return {"tokens": tokens, "proj": proj, "gain": gain, "target": target, "adapter_down_weight": adapter_down_weight, "adapter_up_weight": adapter_up_weight, "source_row_index": source_row_index, "padded_row_index": padded_row_index, "padded_block_tenant": padded_block_tenant}


def owner_slots(source_row_index, padded_row_index, owner_number):
    slot_ids = jnp.arange(SLOTS, dtype=jnp.int32)
    source = slot_ids // CAP
    within = slot_ids % CAP
    local_row = source_row_index[source, owner_number, within]
    global_row = jnp.where(local_row < TOK_DEV, source * TOK_DEV + local_row, TOKENS).astype(jnp.int32)
    global_row = jnp.concatenate([global_row, jnp.full((1,), TOKENS, jnp.int32)])
    return global_row[padded_row_index[owner_number]]

def partial_slots(source_row_index, padded_row_index):

    def one_owner(owner_number):
        return owner_slots(source_row_index, padded_row_index, owner_number)
    return one_owner

def reference(tokens, proj, gain, target, adapter_down_weight, adapter_up_weight, source_row_index, padded_row_index, padded_block_tenant):
    highest = lax.Precision.HIGHEST
    feat_width = MODEL_WIDTH // N_TENSOR
    owner_ids = jnp.arange(N_DP, dtype=jnp.int32)
    padded_rows = jax.vmap(partial_slots(source_row_index, padded_row_index))(owner_ids)
    tenant_numbers = owner_ids[:, None] * TEN_DEV + padded_block_tenant
    tokens_ext = jnp.concatenate([tokens, jnp.zeros((1, MODEL_WIDTH), tokens.dtype)])

    def forward_owner(delta_acc, owner_number):
        rows_here = padded_rows[owner_number]
        feat_padded = tokens_ext[rows_here].reshape(NBLK, BLOCK, MODEL_WIDTH).astype(jnp.float32)
        down_weight_tiles = adapter_down_weight[tenant_numbers[owner_number]].astype(jnp.float32)
        up_weight_tiles = adapter_up_weight[tenant_numbers[owner_number]].astype(jnp.float32)
        rank_act = jnp.einsum('brk,bpk->brp', down_weight_tiles, feat_padded, precision=highest).astype(jnp.bfloat16)
        delta = (2.0 * jnp.einsum('brp,bro->bpo', rank_act.astype(jnp.float32), up_weight_tiles, precision=highest)).astype(jnp.bfloat16)
        delta_acc = delta_acc.at[rows_here].set(delta.reshape(PAD, MODEL_WIDTH))
        return (delta_acc, rank_act)
    delta_rows, rank_all = lax.scan(forward_owner, jnp.zeros((TOKENS + 1, MODEL_WIDTH), jnp.bfloat16), owner_ids)
    delta_rows = delta_rows[:TOKENS]

    def add_block(running, block_id):
        col_start = (block_id * feat_width).astype(jnp.int32)
        x_block = lax.dynamic_slice_in_dim(tokens, col_start, feat_width, 1)
        w_block = lax.dynamic_slice_in_dim(proj, col_start, feat_width, 0)
        partial_value = jnp.dot(x_block, w_block, preferred_element_type=jnp.float32)
        own_cols = lax.dynamic_slice_in_dim(partial_value, col_start, feat_width, 1) + lax.dynamic_slice_in_dim(delta_rows, col_start, feat_width, 1).astype(jnp.float32)
        partial_value = lax.dynamic_update_slice_in_dim(partial_value, own_cols, col_start, 1)
        rounded = lax.optimization_barrier(partial_value.astype(jnp.bfloat16))
        return (running + rounded.astype(jnp.float32), None)
    hidden, _ = lax.scan(add_block, jnp.zeros((TOKENS, MODEL_WIDTH), jnp.float32), jnp.arange(N_TENSOR, dtype=jnp.int32))
    inv_rms = lax.rsqrt(lax.optimization_barrier(jnp.mean(hidden * hidden, axis=1, keepdims=True)) + 1e-05)
    scaled = hidden * inv_rms
    gain_row = gain.astype(jnp.float32)[None, :]
    normed = scaled * gain_row
    draft = normed.astype(jnp.bfloat16)
    weighted = gain_row * ((normed - target.astype(jnp.float32)) / 8.0)
    grad_dot = lax.optimization_barrier(jnp.mean(weighted * scaled, axis=1, keepdims=True))
    grad_hidden = (inv_rms * (weighted - scaled * grad_dot)).astype(jnp.bfloat16)
    grad_ext = jnp.concatenate([grad_hidden, jnp.zeros((1, MODEL_WIDTH), jnp.bfloat16)])

    def backward_owner(owner_number):
        rows_here = padded_rows[owner_number]
        feat_padded = tokens_ext[rows_here].reshape(NBLK, BLOCK, MODEL_WIDTH).astype(jnp.float32)
        grad_padded = grad_ext[rows_here].reshape(NBLK, BLOCK, MODEL_WIDTH).astype(jnp.float32)
        up_weight_tiles = adapter_up_weight[tenant_numbers[owner_number]].astype(jnp.float32)
        rank_act = rank_all[owner_number].astype(jnp.float32)
        onehot = (padded_block_tenant[owner_number][:, None] == jnp.arange(TEN_DEV, dtype=jnp.int32)[None, :]).astype(jnp.float32)
        up_part = 2.0 * jnp.einsum('brp,bpo->bro', rank_act, grad_padded, precision=highest)
        grad_up = jnp.einsum('bt,bro->tro', onehot, up_part, precision=highest).astype(jnp.bfloat16)
        back_act = (2.0 * jnp.einsum('bpo,bro->brp', grad_padded, up_weight_tiles, precision=highest)).astype(jnp.bfloat16)
        down_part = jnp.einsum('brp,bpk->brk', back_act.astype(jnp.float32), feat_padded, precision=highest)
        grad_down = jnp.einsum('bt,brk->trk', onehot, down_part, precision=highest).astype(jnp.bfloat16)
        return (grad_down, grad_up)
    grad_down, grad_up = lax.map(backward_owner, owner_ids)
    return (draft, grad_down.reshape(TENANT_COUNT, ADAPTER_RANK, MODEL_WIDTH), grad_up.reshape(TENANT_COUNT, ADAPTER_RANK, MODEL_WIDTH))
```

```python
import functools

import jax
import jax.numpy as jnp
from jax import lax
from jax.experimental import pallas as pl
from jax.experimental.pallas import tpu as pltpu
from jax.sharding import PartitionSpec as P

MODEL_WIDTH = 8192
MESH = pl.DeviceIdType.MESH
BF = jnp.bfloat16
F32 = jnp.float32
NT = (((1,), (1,)), ((), ()))

N_DP = 16
N_TEN = 16
NZ = 8
CAP = 96
SLOTS = N_DP * CAP
TEN = 16
RANK = 64
ROWS = 512
FEAT = 512
LANES = SLOTS // 4


def aligned(value, multiple):
    return pl.multiple_of(value, multiple)


def kernel(
    tok, proj, gain, target, down, up, rcol, rrow, tcol, trow,
    draft, gdown, gup,
    proj_v, onehot, out_slots, feat, back_slots, gslots, expand, expand_t,
    first, ring, ysend, yrecv, hidden, delta_rows, grad_rows,
    rank_part, rank_land, rank_full, back_part, back_land, back_full,
    stat_send, stat_land,
    proj_sem, a2a_sem, ring_sem, ar_sem, y_sem, stat_sem,
):
    dp = lax.axis_index("dp")
    ten = lax.axis_index("tensor")
    z, y = ten // 2, ten % 2

    barrier = pltpu.get_barrier_semaphore()

    def greet(d, carry):
        pl.semaphore_signal(
            barrier, inc=1, device_id=((dp + d) % N_DP, ten), device_id_type=MESH
        )
        pl.semaphore_signal(
            barrier, inc=1, device_id=(dp, (ten + d) % N_TEN), device_id_type=MESH
        )
        return carry

    lax.fori_loop(1, N_DP, greet, 0)

    def chunk_cols(c):
        return pl.ds(aligned(c * 1024, 1024), 1024)

    def load_proj(c):
        return pltpu.make_async_copy(
            proj.at[:, chunk_cols(c)], proj_v.at[:, chunk_cols(c)], proj_sem.at[c]
        )

    for place in (7, 1, 6, 2, 5, 3, 4, 0):
        load_proj((z + place) % NZ).start()

    for b in range(4):
        rows = pl.ds(b * 384, 384)
        hit = rcol[rows, :] == lax.broadcasted_iota(jnp.int32, (384, ROWS), 1)
        onehot[rows, :] = jnp.where(hit, 1.0, 0.0).astype(BF)

    def to_slots(src):
        def one(b, carry):
            rows = pl.ds(aligned(b * 384, 384), 384)
            out_slots[rows, :] = jnp.dot(
                onehot[rows, :], src[...], preferred_element_type=F32
            ).astype(BF)
            return carry

        lax.fori_loop(0, 4, one, 0)

    def slot_rows(s):
        return pl.ds(aligned(s * CAP, 32), CAP)

    def a2a_copy(src, dst, which, d):
        peer = (dp + d) % N_DP
        return pltpu.make_async_remote_copy(
            src_ref=src.at[slot_rows(peer), :],
            dst_ref=dst.at[slot_rows(dp), :],
            send_sem=a2a_sem.at[which, 0, d - 1],
            recv_sem=a2a_sem.at[which, 1, d - 1],
            device_id=(peer, ten),
            device_id_type=MESH,
        )

    def a2a_start(src, dst, which):
        def one(d, carry):
            a2a_copy(src, dst, which, d).start()
            return carry

        lax.fori_loop(1, N_DP, one, 0)
        dst[slot_rows(dp), :] = src[slot_rows(dp), :]

    def a2a_wait(src, dst, which):
        def one(d, carry):
            a2a_copy(src, dst, which, d).wait()
            return carry

        lax.fori_loop(1, N_DP, one, 0)

    to_slots(tok)
    pl.semaphore_wait(barrier, 2 * (N_DP - 1))
    a2a_start(out_slots, feat, 0)

    def stream_rows(i):
        return pl.ds(aligned(i * 128, 128), 128)

    def sign(i):
        return 1 - 2 * (i % 2)

    def ring_copy(s, i):
        src = first.at[i] if s == 0 else ring.at[s - 1, i]
        peer = ((z + sign(i) + NZ) % NZ) * 2 + y
        return pltpu.make_async_remote_copy(
            src_ref=src,
            dst_ref=ring.at[s, i],
            send_sem=ring_sem.at[0, s, i],
            recv_sem=ring_sem.at[1, s, i],
            device_id=(dp, peer),
            device_id_type=MESH,
        )

    def partial_tile(i, c, j):
        cols = pl.ds(aligned(c * 1024 + j * 512, 512), 512)
        return jnp.dot(
            tok[stream_rows(i), :], proj_v[:, cols], preferred_element_type=F32
        )

    def tile(j):
        return pl.ds(aligned(j * 512, 512), 512)

    def ring_step(s):
        if s == 0:
            load_proj((z + 7) % NZ).wait()
            load_proj((z + 1) % NZ).wait()
        elif s < 3:
            load_proj((z + 7 - s) % NZ).wait()
            load_proj((z + 1 + s) % NZ).wait()
        elif s == 3:
            load_proj((z + 4) % NZ).wait()

        def one(i, carry):
            c = (z + 2 * NZ - sign(i) * (s + 1)) % NZ
            if s:
                ring_copy(s - 1, i).wait_recv()

            def cols(j, carry):
                part = partial_tile(i, c, j)
                if s == 0:
                    first[i, :, tile(j)] = part.astype(BF)
                else:
                    ring[s - 1, i, :, tile(j)] = (
                        part + ring[s - 1, i, :, tile(j)].astype(F32)
                    ).astype(BF)
                return carry

            lax.fori_loop(0, 2, cols, 0)
            ring_copy(s, i).start()
            return carry

        lax.fori_loop(0, 4, one, 0)

    def chunk(arr, t):
        return arr.at[
            pl.ds(aligned((t // 4) * 16, 16), 16), pl.ds(aligned((t % 4) * LANES, 128), LANES)
        ]

    def scatter_copy(part, land, which, d):
        peer = (ten + d) % N_TEN
        return pltpu.make_async_remote_copy(
            src_ref=chunk(part, peer),
            dst_ref=land.at[d - 1],
            send_sem=ar_sem.at[which, 0, d - 1],
            recv_sem=ar_sem.at[which, 1, d - 1],
            device_id=(dp, peer),
            device_id_type=MESH,
        )

    def spread_copy(full, which, d):
        return pltpu.make_async_remote_copy(
            src_ref=chunk(full, ten),
            dst_ref=chunk(full, ten),
            send_sem=ar_sem.at[which, 2, d - 1],
            recv_sem=ar_sem.at[which, 3, d - 1],
            device_id=(dp, (ten + d) % N_TEN),
            device_id_type=MESH,
        )

    def each_peer(action):
        def one(d, carry):
            action(d)
            return carry

        lax.fori_loop(1, N_TEN, one, 0)

    def ar_first(part, land, which):
        each_peer(lambda d: scatter_copy(part, land, which, d).start())

    def ar_second(part, land, full, which):
        each_peer(lambda d: scatter_copy(part, land, which, d).wait())
        total = chunk(part, ten)[...].astype(F32)
        for d in range(N_TEN - 1):
            total = total + land[d].astype(F32)
        chunk(full, ten)[...] = total.astype(BF)
        each_peer(lambda d: spread_copy(full, which, d).start())

    def ar_wait(full, which):
        each_peer(lambda d: spread_copy(full, which, d).wait())

    def low_rank(weights, rows_ref, scale, out):
        def one(j, carry):
            lanes = pl.ds(aligned(j * 256, 256), 256)
            full = lax.dot_general(
                weights[...], rows_ref[lanes, :], NT, preferred_element_type=F32
            )
            tenant = jnp.broadcast_to(trow[:, lanes], (RANK, 256))
            total = jnp.zeros((RANK, 256), F32)
            for t in range(TEN):
                total = total + jnp.where(
                    tenant == t, full[t * RANK : (t + 1) * RANK, :], 0.0
                )
            out[:, lanes] = (scale * total).astype(BF)
            return carry

        lax.fori_loop(0, SLOTS // 256, one, 0)

    def spread_tenants(full):
        def one(j, carry):
            lanes = pl.ds(aligned(j * 256, 256), 256)
            value = full[:, lanes].astype(F32)
            tenant = jnp.broadcast_to(trow[:, lanes], (RANK, 256))
            for t in range(TEN):
                expand_t[t * RANK : (t + 1) * RANK, lanes] = jnp.where(
                    tenant == t, value, 0.0
                ).astype(BF)
            return carry

        lax.fori_loop(0, SLOTS // 256, one, 0)

    def grouped_outer(rows_ref, scale, out):
        def one(t, carry):
            rows = pl.ds(aligned(t * 256, 256), 256)
            out[rows, :] = (
                scale
                * jnp.dot(expand_t[rows, :], rows_ref[...], preferred_element_type=F32)
            ).astype(BF)
            return carry

        lax.fori_loop(0, TEN * RANK // 256, one, 0)

    ring_step(0)
    ring_step(1)

    a2a_wait(out_slots, feat, 0)
    low_rank(down, feat, 1.0, rank_part)
    ar_first(rank_part, rank_land, 0)

    ring_step(2)

    ar_second(rank_part, rank_land, rank_full, 0)

    ring_step(3)

    ar_wait(rank_full, 0)

    def deltas(b, carry):
        rows = pl.ds(aligned(b * 256, 256), 256)
        value = rank_full[:, rows].astype(F32)
        twice = jnp.concatenate([value, value], axis=0).T
        lane = lax.broadcasted_iota(jnp.int32, (256, 128), 1)
        tenant = jnp.broadcast_to(tcol[rows, :], (256, 128)) - jnp.where(
            lane >= RANK, 1, 0
        )
        for j in range(TEN // 2):
            expand[:, j * 128 : (j + 1) * 128] = jnp.where(
                tenant == 2 * j, twice, 0.0
            ).astype(BF)
        out_slots[rows, :] = (
            2.0 * jnp.dot(expand[...], up[...], preferred_element_type=F32)
        ).astype(BF)
        return carry

    lax.fori_loop(0, SLOTS // 256, deltas, 0)
    a2a_start(out_slots, back_slots, 1)

    ring_step(4)

    spread_tenants(rank_full)

    ring_step(5)
    ring_step(6)

    a2a_wait(out_slots, back_slots, 1)

    def scatter_rows(b, carry):
        rows = pl.ds(aligned(b * 128, 128), 128)
        hit = lax.broadcasted_iota(jnp.int32, (128, SLOTS), 0) + b * 128 == (
            jnp.broadcast_to(rrow[...], (128, SLOTS))
        )
        delta_rows[rows, :] = jnp.dot(
            jnp.where(hit, 1.0, 0.0).astype(BF),
            back_slots[...],
            preferred_element_type=F32,
        )
        return carry

    lax.fori_loop(0, 4, scatter_rows, 0)

    load_proj(z).wait()

    def y_copy(i):
        return pltpu.make_async_remote_copy(
            src_ref=ysend.at[i],
            dst_ref=yrecv.at[i],
            send_sem=y_sem.at[0, i],
            recv_sem=y_sem.at[1, i],
            device_id=(dp, z * 2 + 1 - y),
            device_id_type=MESH,
        )

    def last_hop(i, carry):
        ring_copy(6, i).wait_recv()
        ysend[i] = (
            partial_tile(i, z, 1 - y) + ring[6, i, :, tile(1 - y)].astype(F32)
        ).astype(BF)
        y_copy(i).start()
        hidden[stream_rows(i), :] = (
            partial_tile(i, z, y)
            + ring[6, i, :, tile(y)].astype(F32)
            + delta_rows[stream_rows(i), :]
        )
        return carry

    lax.fori_loop(0, 4, last_hop, 0)

    def stats(i, carry):
        y_copy(i).wait()
        rows = stream_rows(i)
        h = hidden[rows, :] + yrecv[i].astype(F32)
        hidden[rows, :] = h
        g = gain[...]
        gh = g * h
        s1 = jnp.sum(h * h, axis=1, keepdims=True)
        s2 = jnp.sum(gh * gh, axis=1, keepdims=True)
        s3 = jnp.sum(gh * target[rows, :].astype(F32), axis=1, keepdims=True)
        lane = lax.broadcasted_iota(jnp.int32, (128, 128), 1)
        table = jnp.where(lane == 0, s1, jnp.where(lane == 1, s2, s3))
        stat_send[i] = table.T[0:8, :]
        return carry

    lax.fori_loop(0, 4, stats, 0)

    def stat_copy(d):
        return pltpu.make_async_remote_copy(
            src_ref=stat_send,
            dst_ref=stat_land.at[d - 1],
            send_sem=stat_sem.at[0, d - 1],
            recv_sem=stat_sem.at[1, d - 1],
            device_id=(dp, (ten + d) % N_TEN),
            device_id_type=MESH,
        )

    each_peer(lambda d: stat_copy(d).start())
    each_peer(lambda d: stat_copy(d).wait())

    def grads(i, carry):
        total = stat_send[i]
        for d in range(N_TEN - 1):
            total = total + stat_land[d, i]
        table = jnp.concatenate([total, jnp.zeros((120, 128), F32)], axis=0).T
        rows = stream_rows(i)
        inv = lax.rsqrt(table[:, 0:1] / MODEL_WIDTH + 1e-05)
        dot = inv * (inv * table[:, 1:2] - table[:, 2:3]) / 8.0
        g = gain[...]
        scaled = hidden[rows, :] * inv
        normed = scaled * g
        draft[rows, :] = normed.astype(BF)
        weighted = g * ((normed - target[rows, :].astype(F32)) / 8.0)
        grad_rows[rows, :] = (inv * (weighted - scaled * (dot / MODEL_WIDTH))).astype(BF)
        return carry

    lax.fori_loop(0, 4, grads, 0)

    to_slots(grad_rows)
    a2a_start(out_slots, gslots, 2)
    a2a_wait(out_slots, gslots, 2)
    low_rank(up, gslots, 2.0, back_part)
    ar_first(back_part, back_land, 1)
    ar_second(back_part, back_land, back_full, 1)
    grouped_outer(gslots, 2.0, gup)
    ar_wait(back_full, 1)
    spread_tenants(back_full)
    grouped_outer(feat, 1.0, gdown)

    for s in range(NZ - 1):

        def drain(i, carry, s=s):
            ring_copy(s, i).wait_send()
            return carry

        lax.fori_loop(0, 4, drain, 0)


def slot_tenants(positions, block_tenant):
    tenant = jnp.repeat(block_tenant, positions.shape[0] // block_tenant.shape[0]) + 1
    high = positions[None, :] // 64 == jnp.arange(SLOTS // 64, dtype=jnp.int32)[:, None]
    low = positions[:, None] % 64 == jnp.arange(64, dtype=jnp.int32)[None, :]
    table = jnp.dot(
        high.astype(BF),
        jnp.where(low, tenant[:, None], 0).astype(BF),
        preferred_element_type=F32,
    )
    return table.reshape(SLOTS).astype(jnp.int32) - 1


def body(
    tokens,
    proj,
    gain,
    target,
    adapter_down_weight,
    adapter_up_weight,
    source_row_index,
    padded_row_index,
    padded_block_tenant,
):
    routes = source_row_index[0].reshape(SLOTS)
    tenants = slot_tenants(padded_row_index[0], padded_block_tenant[0])
    vmem = pl.BlockSpec(memory_space=pltpu.VMEM)
    wide = TEN * RANK
    draft, grad_down, grad_up = pl.pallas_call(
        kernel,
        out_shape=(
            jax.ShapeDtypeStruct((ROWS, FEAT), BF),
            jax.ShapeDtypeStruct((wide, FEAT), BF),
            jax.ShapeDtypeStruct((wide, FEAT), BF),
        ),
        in_specs=[vmem, pl.BlockSpec(memory_space=pl.ANY)] + [vmem] * 8,
        out_specs=(vmem, vmem, vmem),
        scratch_shapes=[
            pltpu.VMEM((FEAT, MODEL_WIDTH), BF),
            pltpu.VMEM((SLOTS, ROWS), BF),
            pltpu.VMEM((SLOTS, FEAT), BF),
            pltpu.VMEM((SLOTS, FEAT), BF),
            pltpu.VMEM((SLOTS, FEAT), BF),
            pltpu.VMEM((SLOTS, FEAT), BF),
            pltpu.VMEM((256, wide), BF),
            pltpu.VMEM((wide, SLOTS), BF),
            pltpu.VMEM((4, 128, 1024), BF),
            pltpu.VMEM((NZ - 1, 4, 128, 1024), BF),
            pltpu.VMEM((4, 128, FEAT), BF),
            pltpu.VMEM((4, 128, FEAT), BF),
            pltpu.VMEM((ROWS, FEAT), F32),
            pltpu.VMEM((ROWS, FEAT), F32),
            pltpu.VMEM((ROWS, FEAT), BF),
            pltpu.VMEM((RANK, SLOTS), BF),
            pltpu.VMEM((N_TEN - 1, 16, LANES), BF),
            pltpu.VMEM((RANK, SLOTS), BF),
            pltpu.VMEM((RANK, SLOTS), BF),
            pltpu.VMEM((N_TEN - 1, 16, LANES), BF),
            pltpu.VMEM((RANK, SLOTS), BF),
            pltpu.VMEM((4, 8, 128), F32),
            pltpu.VMEM((N_TEN - 1, 4, 8, 128), F32),
            pltpu.SemaphoreType.DMA((NZ,)),
            pltpu.SemaphoreType.DMA((3, 2, N_DP - 1)),
            pltpu.SemaphoreType.DMA((2, NZ - 1, 4)),
            pltpu.SemaphoreType.DMA((2, 4, N_TEN - 1)),
            pltpu.SemaphoreType.DMA((2, 4)),
            pltpu.SemaphoreType.DMA((2, N_TEN - 1)),
        ],
        compiler_params=pltpu.CompilerParams(
            collective_id=0, has_side_effects=True, vmem_limit_bytes=58 << 20
        ),
        name="step",
    )(
        tokens,
        proj,
        gain.reshape(1, FEAT),
        target,
        adapter_down_weight.reshape(wide, FEAT),
        adapter_up_weight.reshape(wide, FEAT),
        routes.reshape(SLOTS, 1),
        routes.reshape(1, SLOTS),
        tenants.reshape(SLOTS, 1),
        tenants.reshape(1, SLOTS),
    )
    return (
        draft,
        grad_down.reshape(TEN, RANK, FEAT),
        grad_up.reshape(TEN, RANK, FEAT),
    )


def solution(mesh):
    return jax.shard_map(
        body,
        mesh=mesh,
        in_specs=(
            P("dp", "tensor"),
            P("tensor", None),
            P("tensor"),
            P("dp", "tensor"),
            P("dp", None, "tensor"),
            P("dp", None, "tensor"),
            P("dp", None, None),
            P("dp", None),
            P("dp", None),
        ),
        out_specs=(P("dp", "tensor"), P("dp", None, "tensor"), P("dp", None, "tensor")),
        check_vma=False,
    )
```

```python
import jax
import jax.numpy as jnp
from jax import lax
from jax.experimental import pallas as pl
from jax.experimental.pallas import tpu as pltpu
from jax.sharding import PartitionSpec as P

MODEL_WIDTH = 8192
MESH = pl.DeviceIdType.MESH
BF = jnp.bfloat16
F32 = jnp.float32
NT = (((1,), (1,)), ((), ()))
TN = (((0,), (0,)), ((), ()))

N_DP = 16
N_TEN = 16
NZ = 8
CAP = 96
SLOTS = N_DP * CAP
TEN = 16
RANK = 64
ROWS = 512
FEAT = 512
LANES = SLOTS // 4
PHASES = 2
WIDE = FEAT // PHASES


def aligned(value, multiple):
    return pl.multiple_of(value, multiple)


def kernel(
    tok, proj, gain, target, down, up, routes, positions, blocks,
    draft, gdown, gup,
    proj_v, onehot, tok_out, tgt_out, delta_out, h_out, feat, tgt_slots,
    back_slots, h_slots, gslots, expand, expand_t,
    first, ring, ysend, yrecv, hidden, delta_rows, h_rows,
    rank_part, rank_land, rank_full, back_part, back_land, back_full,
    trow, tcol, stat_send, stat_land, scal_send, scal_land,
    proj_sem, a2a_sem, h_sem, scal_sem, ring_sem, ar_sem, y_sem, stat_sem,
):
    dp = lax.axis_index("dp")
    ten = lax.axis_index("tensor")
    z, y = ten // 2, ten % 2

    barrier = pltpu.get_barrier_semaphore()

    def greet(d, carry):
        pl.semaphore_signal(
            barrier, inc=1, device_id=((dp + d) % N_DP, ten), device_id_type=MESH
        )
        pl.semaphore_signal(
            barrier, inc=1, device_id=(dp, (ten + d) % N_TEN), device_id_type=MESH
        )
        return carry

    lax.fori_loop(1, N_DP, greet, 0)

    def chunk_cols(c):
        return pl.ds(aligned(c * 1024, 1024), 1024)

    def load_proj(c):
        return pltpu.make_async_copy(
            proj.at[:, chunk_cols(c)], proj_v.at[:, chunk_cols(c)], proj_sem.at[c]
        )

    for place in (7, 1, 6, 2, 5, 3, 4, 0):
        load_proj((z + place) % NZ).start()

    route = jnp.concatenate(
        [routes[0].astype(F32), jnp.zeros((N_DP, 128 - CAP), F32)], axis=1
    )
    route = jnp.concatenate([route, jnp.zeros((128 - N_DP, 128), F32)], axis=0).T
    row_number = lax.broadcasted_iota(jnp.int32, (CAP, ROWS), 1).astype(F32)
    for d in range(N_DP):
        hit = jnp.broadcast_to(route[0:CAP, d : d + 1], (CAP, ROWS)) == row_number
        onehot[d * CAP : (d + 1) * CAP, :] = jnp.where(hit, 1.0, 0.0).astype(BF)

    def to_slots(src, dst):
        def one(b, carry):
            rows = pl.ds(aligned(b * 384, 384), 384)
            dst[rows, :] = jnp.dot(
                onehot[rows, :], src[...], preferred_element_type=F32
            ).astype(BF)
            return carry

        lax.fori_loop(0, 4, one, 0)

    def slot_rows(s):
        return pl.ds(aligned(s * CAP, 32), CAP)

    def a2a_copy(src, dst, sems, d):
        peer = (dp + d) % N_DP
        return pltpu.make_async_remote_copy(
            src_ref=src.at[slot_rows(peer), :],
            dst_ref=dst.at[slot_rows(dp), :],
            send_sem=sems.at[0, d - 1],
            recv_sem=sems.at[1, d - 1],
            device_id=(peer, ten),
            device_id_type=MESH,
        )

    def each_peer(action):
        def one(d, carry):
            action(d)
            return carry

        lax.fori_loop(1, N_TEN, one, 0)

    def a2a_start(src, dst, sems):
        each_peer(lambda d: a2a_copy(src, dst, sems, d).start())
        dst[slot_rows(dp), :] = src[slot_rows(dp), :]

    def a2a_wait(src, dst, sems):
        each_peer(lambda d: a2a_copy(src, dst, sems, d).wait())

    to_slots(tok, tok_out)
    pl.semaphore_wait(barrier, 2 * (N_DP - 1))
    a2a_start(tok_out, feat, a2a_sem.at[0])

    def stream_rows(i):
        return pl.ds(aligned(i * 128, 128), 128)

    def sign(i):
        return 1 - 2 * (i % 2)

    def ring_copy(p, s, i):
        src = first.at[p, i] if s == 0 else ring.at[p, s - 1, i]
        peer = ((z + sign(i) + NZ) % NZ) * 2 + y
        return pltpu.make_async_remote_copy(
            src_ref=src,
            dst_ref=ring.at[p, s, i],
            send_sem=ring_sem.at[0, p, s, i],
            recv_sem=ring_sem.at[1, p, s, i],
            device_id=(dp, peer),
            device_id_type=MESH,
        )

    def partial_tile(p, i, c, j):
        cols = pl.ds(aligned(c * 1024 + j * 512 + p * WIDE, 128), WIDE)
        return jnp.dot(
            tok[stream_rows(i), :], proj_v[:, cols], preferred_element_type=F32
        )

    def ring_step(p, s):
        if p == 0 and s == 0:
            load_proj((z + 7) % NZ).wait()
            load_proj((z + 1) % NZ).wait()
        elif p == 0 and s < 3:
            load_proj((z + 7 - s) % NZ).wait()
            load_proj((z + 1 + s) % NZ).wait()
        elif p == 0 and s == 3:
            load_proj((z + 4) % NZ).wait()

        def one(i, carry):
            c = (z + 2 * NZ - sign(i) * (s + 1)) % NZ
            if s:
                ring_copy(p, s - 1, i).wait_recv()
            for j in range(2):
                part = partial_tile(p, i, c, j)
                cols = pl.ds(j * WIDE, WIDE)
                if s == 0:
                    first[p, i, :, cols] = part.astype(BF)
                else:
                    ring[p, s - 1, i, :, cols] = (
                        part + ring[p, s - 1, i, :, cols].astype(F32)
                    ).astype(BF)
            ring_copy(p, s, i).start()
            return carry

        lax.fori_loop(0, 4, one, 0)

    def y_copy(p, i):
        return pltpu.make_async_remote_copy(
            src_ref=ysend.at[p, i],
            dst_ref=yrecv.at[p, i],
            send_sem=y_sem.at[0, p, i],
            recv_sem=y_sem.at[1, p, i],
            device_id=(dp, z * 2 + 1 - y),
            device_id_type=MESH,
        )

    def half(j):
        return pl.ds(aligned(j * WIDE, 128), WIDE)

    def last_hop(p):
        if p == 0:
            load_proj(z).wait()

        def one(i, carry):
            ring_copy(p, NZ - 2, i).wait_recv()
            ysend[p, i] = (
                partial_tile(p, i, z, 1 - y)
                + ring[p, NZ - 2, i, :, half(1 - y)].astype(F32)
            ).astype(BF)
            y_copy(p, i).start()
            hidden[p, stream_rows(i), :] = partial_tile(p, i, z, y) + ring[
                p, NZ - 2, i, :, half(y)
            ].astype(F32)
            return carry

        lax.fori_loop(0, 4, one, 0)

    def finish(p):
        def one(i, carry):
            y_copy(p, i).wait()
            rows = stream_rows(i)
            total = hidden[p, rows, :] + yrecv[p, i].astype(F32)
            hidden[p, rows, :] = total
            h_rows[rows, :] = total.astype(BF)
            return carry

        lax.fori_loop(0, 4, one, 0)
        to_slots(h_rows, h_out.at[p])
        a2a_start(h_out.at[p], h_slots.at[p], h_sem.at[p])

    def chunk(arr, t):
        return arr.at[
            pl.ds(aligned((t // 4) * 16, 16), 16), pl.ds(aligned((t % 4) * LANES, 128), LANES)
        ]

    def scatter_copy(part, land, which, d):
        peer = (ten + d) % N_TEN
        return pltpu.make_async_remote_copy(
            src_ref=chunk(part, peer),
            dst_ref=land.at[d - 1],
            send_sem=ar_sem.at[which, 0, d - 1],
            recv_sem=ar_sem.at[which, 1, d - 1],
            device_id=(dp, peer),
            device_id_type=MESH,
        )

    def spread_copy(full, which, d):
        return pltpu.make_async_remote_copy(
            src_ref=chunk(full, ten),
            dst_ref=chunk(full, ten),
            send_sem=ar_sem.at[which, 2, d - 1],
            recv_sem=ar_sem.at[which, 3, d - 1],
            device_id=(dp, (ten + d) % N_TEN),
            device_id_type=MESH,
        )

    def ar_first(part, land, which):
        each_peer(lambda d: scatter_copy(part, land, which, d).start())

    def ar_second(part, land, full, which):
        each_peer(lambda d: scatter_copy(part, land, which, d).wait())
        total = chunk(part, ten)[...].astype(F32)
        for d in range(N_TEN - 1):
            total = total + land[d].astype(F32)
        chunk(full, ten)[...] = total.astype(BF)
        each_peer(lambda d: spread_copy(full, which, d).start())

    def ar_wait(full, which):
        each_peer(lambda d: spread_copy(full, which, d).wait())

    def low_rank(weights, rows_ref, scale, out):
        def one(j, carry):
            lanes = pl.ds(aligned(j * 256, 256), 256)
            full = lax.dot_general(
                weights[...], rows_ref[lanes, :], NT, preferred_element_type=F32
            )
            tenant = jnp.broadcast_to(trow[:, lanes], (RANK, 256))
            total = jnp.zeros((RANK, 256), F32)
            for t in range(TEN):
                total = total + jnp.where(
                    tenant == t + 1.0, full[t * RANK : (t + 1) * RANK, :], 0.0
                )
            out[:, lanes] = (scale * total).astype(BF)
            return carry

        lax.fori_loop(0, SLOTS // 256, one, 0)

    def spread_tenants(full):
        def one(j, carry):
            lanes = pl.ds(aligned(j * 256, 256), 256)
            value = full[:, lanes].astype(F32)
            tenant = jnp.broadcast_to(trow[:, lanes], (RANK, 256))
            for t in range(TEN):
                expand_t[t * RANK : (t + 1) * RANK, lanes] = jnp.where(
                    tenant == t + 1.0, value, 0.0
                ).astype(BF)
            return carry

        lax.fori_loop(0, SLOTS // 256, one, 0)

    def grouped_outer(rows_ref, scale, out):
        def one(t, carry):
            rows = pl.ds(aligned(t * 256, 256), 256)
            out[rows, :] = (
                scale
                * jnp.dot(expand_t[rows, :], rows_ref[...], preferred_element_type=F32)
            ).astype(BF)
            return carry

        lax.fori_loop(0, TEN * RANK // 256, one, 0)

    def slot_tenants():
        held = positions[...]
        count = held.shape[1]
        owner = jnp.concatenate(
            [
                jnp.broadcast_to(blocks[:, b : b + 1].astype(F32) + 1.0, (1, 128))
                for b in range(count // 128)
            ],
            axis=1,
        )
        high = jnp.where(
            jnp.broadcast_to(held // 128, (16, count))
            == lax.broadcasted_iota(jnp.int32, (16, count), 0),
            1.0,
            0.0,
        ).astype(BF)
        low = jnp.where(
            jnp.broadcast_to(held % 128, (128, count))
            == lax.broadcasted_iota(jnp.int32, (128, count), 0),
            jnp.broadcast_to(owner, (128, count)),
            0.0,
        ).astype(BF)
        table = lax.dot_general(high, low, NT, preferred_element_type=F32)
        columns = jnp.concatenate([table, jnp.zeros((112, 128), F32)], axis=0).T
        for a in range(SLOTS // 128):
            trow[:, a * 128 : (a + 1) * 128] = table[a : a + 1, :]
            tcol[a * 128 : (a + 1) * 128, :] = jnp.broadcast_to(
                columns[:, a : a + 1], (128, 128)
            )

    def deltas(b, carry):
        rows = pl.ds(aligned(b * 256, 256), 256)
        value = rank_full[:, rows].astype(F32)
        twice = jnp.concatenate([value, value], axis=0).T
        lane = lax.broadcasted_iota(jnp.int32, (256, 128), 1)
        tenant = tcol[rows, :] - jnp.where(lane >= RANK, 1.0, 0.0)
        for j in range(TEN // 2):
            expand[:, j * 128 : (j + 1) * 128] = jnp.where(
                tenant == 2.0 * j + 1.0, twice, 0.0
            ).astype(BF)
        delta_out[rows, :] = (
            2.0 * jnp.dot(expand[...], up[...], preferred_element_type=F32)
        ).astype(BF)
        return carry

    def scatter_rows():
        for q in range(4):
            cols = pl.ds(q * 128, 128)
            delta_rows[cols, :] = lax.dot_general(
                onehot[:, cols], back_slots[...], TN, preferred_element_type=F32
            )

    ring_step(0, 0)
    slot_tenants()
    to_slots(target, tgt_out)
    ring_step(0, 1)
    ring_step(0, 2)
    ring_step(0, 3)
    a2a_wait(tok_out, feat, a2a_sem.at[0])
    low_rank(down, feat, 1.0, rank_part)
    ar_first(rank_part, rank_land, 0)
    a2a_start(tgt_out, tgt_slots, a2a_sem.at[2])
    ring_step(0, 4)
    ring_step(0, 5)
    ar_second(rank_part, rank_land, rank_full, 0)
    ring_step(0, 6)
    ring_step(1, 0)
    last_hop(0)
    ring_step(1, 1)
    ar_wait(rank_full, 0)
    lax.fori_loop(0, SLOTS // 256, deltas, 0)
    a2a_start(delta_out, back_slots, a2a_sem.at[1])
    ring_step(1, 2)
    finish(0)
    ring_step(1, 3)
    spread_tenants(rank_full)
    ring_step(1, 4)
    ring_step(1, 5)
    ring_step(1, 6)
    a2a_wait(delta_out, back_slots, a2a_sem.at[1])
    scatter_rows()
    last_hop(1)
    finish(1)

    for i in range(4):
        rows = pl.ds(i * 128, 128)
        s1 = jnp.zeros((128, 1), F32)
        s2 = jnp.zeros((128, 1), F32)
        s3 = jnp.zeros((128, 1), F32)
        for p in range(PHASES):
            cols = pl.ds(p * WIDE, WIDE)
            h = hidden[p, rows, :] + delta_rows[rows, cols]
            hidden[p, rows, :] = h
            gh = gain[:, cols] * h
            s1 += jnp.sum(h * h, axis=1, keepdims=True)
            s2 += jnp.sum(gh * gh, axis=1, keepdims=True)
            s3 += jnp.sum(gh * target[rows, cols].astype(F32), axis=1, keepdims=True)
        lane = lax.broadcasted_iota(jnp.int32, (128, 128), 1)
        table = jnp.where(lane == 0, s1, jnp.where(lane == 1, s2, s3))
        stat_send[4 * i : 4 * i + 4, :] = table.T[0:4, :]

    def stat_copy(d):
        return pltpu.make_async_remote_copy(
            src_ref=stat_send,
            dst_ref=stat_land.at[d - 1],
            send_sem=stat_sem.at[0, d - 1],
            recv_sem=stat_sem.at[1, d - 1],
            device_id=(dp, (ten + d) % N_TEN),
            device_id_type=MESH,
        )

    each_peer(lambda d: stat_copy(d).start())
    each_peer(lambda d: stat_copy(d).wait())

    total = stat_send[...]
    for d in range(N_TEN - 1):
        total = total + stat_land[d]
    invs, dots = [], []
    for i in range(4):
        s1, s2, s3 = (total[4 * i + q : 4 * i + q + 1, :] for q in range(3))
        inv = lax.rsqrt(s1 / MODEL_WIDTH + 1e-05)
        invs.append(inv)
        dots.append(inv * (inv * s2 - s3) / (8.0 * MODEL_WIDTH))
    scalars = jnp.concatenate(
        [
            jnp.concatenate(invs, axis=1),
            jnp.concatenate(dots, axis=1),
            jnp.zeros((6, ROWS), F32),
        ],
        axis=0,
    )

    for d in range(N_DP):
        scal_send[d, :, 0:CAP] = lax.dot_general(
            scalars,
            onehot[d * CAP : (d + 1) * CAP, :].astype(F32),
            NT,
            precision=lax.Precision.HIGHEST,
            preferred_element_type=F32,
        )
        scal_send[d, :, CAP:128] = jnp.zeros((8, 128 - CAP), F32)

    def scal_copy(d):
        peer = (dp + d) % N_DP
        return pltpu.make_async_remote_copy(
            src_ref=scal_send.at[peer],
            dst_ref=scal_land.at[dp],
            send_sem=scal_sem.at[0, d - 1],
            recv_sem=scal_sem.at[1, d - 1],
            device_id=(peer, ten),
            device_id_type=MESH,
        )

    each_peer(lambda d: scal_copy(d).start())
    scal_land[dp] = scal_send[dp]

    for i in range(4):
        rows = pl.ds(i * 128, 128)
        table = jnp.concatenate([invs[i], jnp.zeros((127, 128), F32)], axis=0).T
        inv = table[:, 0:1]
        for p in range(PHASES):
            cols = pl.ds(p * WIDE, WIDE)
            draft[rows, cols] = (hidden[p, rows, :] * inv * gain[:, cols]).astype(BF)

    a2a_wait(tgt_out, tgt_slots, a2a_sem.at[2])
    for p in range(PHASES):
        a2a_wait(h_out.at[p], h_slots.at[p], h_sem.at[p])
    each_peer(lambda d: scal_copy(d).wait())

    def grads(s, carry):
        rows = slot_rows(s)
        table = jnp.concatenate([scal_land[s], jnp.zeros((120, 128), F32)], axis=0).T
        inv, dot = table[0:CAP, 0:1], table[0:CAP, 1:2]
        for p in range(PHASES):
            cols = pl.ds(p * WIDE, WIDE)
            g = gain[:, cols]
            h = h_slots[p, rows, :].astype(F32) + delta_out[rows, cols].astype(F32)
            scaled = h * inv
            weighted = g * ((scaled * g - tgt_slots[rows, cols].astype(F32)) / 8.0)
            gslots[rows, cols] = (inv * (weighted - scaled * dot)).astype(BF)
        return carry

    lax.fori_loop(0, N_DP, grads, 0)

    low_rank(up, gslots, 2.0, back_part)
    ar_first(back_part, back_land, 1)
    ar_second(back_part, back_land, back_full, 1)
    grouped_outer(gslots, 2.0, gup)
    ar_wait(back_full, 1)
    spread_tenants(back_full)
    grouped_outer(feat, 1.0, gdown)

    for p in range(PHASES):
        for s in range(NZ - 1):

            def drain(i, carry, p=p, s=s):
                ring_copy(p, s, i).wait_send()
                return carry

            lax.fori_loop(0, 4, drain, 0)


def body(
    tokens,
    proj,
    gain,
    target,
    adapter_down_weight,
    adapter_up_weight,
    source_row_index,
    padded_row_index,
    padded_block_tenant,
):
    vmem = pl.BlockSpec(memory_space=pltpu.VMEM)
    wide = TEN * RANK
    dma = pltpu.SemaphoreType.DMA
    draft, grad_down, grad_up = pl.pallas_call(
        kernel,
        out_shape=(
            jax.ShapeDtypeStruct((ROWS, FEAT), BF),
            jax.ShapeDtypeStruct((wide, FEAT), BF),
            jax.ShapeDtypeStruct((wide, FEAT), BF),
        ),
        in_specs=[vmem, pl.BlockSpec(memory_space=pl.ANY)] + [vmem] * 7,
        out_specs=(vmem, vmem, vmem),
        scratch_shapes=[
            pltpu.VMEM((FEAT, MODEL_WIDTH), BF),
            pltpu.VMEM((SLOTS, ROWS), BF),
            pltpu.VMEM((SLOTS, FEAT), BF),
            pltpu.VMEM((SLOTS, FEAT), BF),
            pltpu.VMEM((SLOTS, FEAT), BF),
            pltpu.VMEM((PHASES, SLOTS, WIDE), BF),
            pltpu.VMEM((SLOTS, FEAT), BF),
            pltpu.VMEM((SLOTS, FEAT), BF),
            pltpu.VMEM((SLOTS, FEAT), BF),
            pltpu.VMEM((PHASES, SLOTS, WIDE), BF),
            pltpu.VMEM((SLOTS, FEAT), BF),
            pltpu.VMEM((256, wide), BF),
            pltpu.VMEM((wide, SLOTS), BF),
            pltpu.VMEM((PHASES, 4, 128, 2 * WIDE), BF),
            pltpu.VMEM((PHASES, NZ - 1, 4, 128, 2 * WIDE), BF),
            pltpu.VMEM((PHASES, 4, 128, WIDE), BF),
            pltpu.VMEM((PHASES, 4, 128, WIDE), BF),
            pltpu.VMEM((PHASES, ROWS, WIDE), F32),
            pltpu.VMEM((ROWS, FEAT), F32),
            pltpu.VMEM((ROWS, WIDE), BF),
            pltpu.VMEM((RANK, SLOTS), BF),
            pltpu.VMEM((N_TEN - 1, 16, LANES), BF),
            pltpu.VMEM((RANK, SLOTS), BF),
            pltpu.VMEM((RANK, SLOTS), BF),
            pltpu.VMEM((N_TEN - 1, 16, LANES), BF),
            pltpu.VMEM((RANK, SLOTS), BF),
            pltpu.VMEM((1, SLOTS), F32),
            pltpu.VMEM((SLOTS, 128), F32),
            pltpu.VMEM((16, 128), F32),
            pltpu.VMEM((N_TEN - 1, 16, 128), F32),
            pltpu.VMEM((N_DP, 8, 128), F32),
            pltpu.VMEM((N_DP, 8, 128), F32),
            dma((NZ,)),
            dma((3, 2, N_DP - 1)),
            dma((PHASES, 2, N_DP - 1)),
            dma((2, N_DP - 1)),
            dma((2, PHASES, NZ - 1, 4)),
            dma((2, 4, N_TEN - 1)),
            dma((2, PHASES, 4)),
            dma((2, N_TEN - 1)),
        ],
        compiler_params=pltpu.CompilerParams(
            collective_id=0, has_side_effects=True, vmem_limit_bytes=58 << 20
        ),
        name="step",
    )(
        tokens,
        proj,
        gain.reshape(1, FEAT),
        target,
        adapter_down_weight.reshape(wide, FEAT),
        adapter_up_weight.reshape(wide, FEAT),
        source_row_index,
        padded_row_index,
        padded_block_tenant,
    )
    return (
        draft,
        grad_down.reshape(TEN, RANK, FEAT),
        grad_up.reshape(TEN, RANK, FEAT),
    )


def solution(mesh):
    return jax.shard_map(
        body,
        mesh=mesh,
        in_specs=(
            P("dp", "tensor"),
            P("tensor", None),
            P("tensor"),
            P("dp", "tensor"),
            P("dp", None, "tensor"),
            P("dp", None, "tensor"),
            P("dp", None, None),
            P("dp", None),
            P("dp", None),
        ),
        out_specs=(P("dp", "tensor"), P("dp", None, "tensor"), P("dp", None, "tensor")),
        check_vma=False,
    )
```

```python
import jax
import jax.numpy as jnp
from jax import lax
from jax.experimental import pallas as pl
from jax.experimental.pallas import tpu as pltpu
from jax.sharding import PartitionSpec as P

MODEL_WIDTH = 8192
MESH = pl.DeviceIdType.MESH
BF = jnp.bfloat16
F32 = jnp.float32
NT = (((1,), (1,)), ((), ()))
TN = (((0,), (0,)), ((), ()))

N_DP = 16
N_TEN = 16
NZ = 8
CAP = 96
SLOTS = N_DP * CAP
TEN = 16
RANK = 64
ROWS = 512
FEAT = 512
LANES = SLOTS // 4
PHASES = ((0, 384), (384, 128))


def aligned(value, multiple):
    return pl.multiple_of(value, multiple)


def kernel(
    tok, proj, gain, target, down, up, routes, positions, blocks,
    draft, gdown, gup,
    proj_v, onehot, tok_out, tgt_out, delta_out, h_out, feat, tgt_slots,
    back_slots, h_slots, gslots, expand, expand_t,
    part, first, ring, ysend, yrecv, hidden, delta_rows, h_rows,
    rank_part, rank_land, rank_full, back_part, back_land, back_full,
    trow, tcol, stat_acc, stat_send, stat_land, scal_send, scal_land,
    proj_sem, a2a_sem, h_sem, scal_sem, ring_sem, ar_sem, y_sem, stat_sem,
):
    dp = lax.axis_index("dp")
    ten = lax.axis_index("tensor")
    z, y = ten // 2, ten % 2

    barrier = pltpu.get_barrier_semaphore()

    def greet(d, carry):
        pl.semaphore_signal(
            barrier, inc=1, device_id=((dp + d) % N_DP, ten), device_id_type=MESH
        )
        pl.semaphore_signal(
            barrier, inc=1, device_id=(dp, (ten + d) % N_TEN), device_id_type=MESH
        )
        return carry

    lax.fori_loop(1, N_DP, greet, 0)

    def chunk_cols(c):
        return pl.ds(aligned(c * 1024, 1024), 1024)

    def load_proj(c):
        return pltpu.make_async_copy(
            proj.at[:, chunk_cols(c)], proj_v.at[:, chunk_cols(c)], proj_sem.at[c]
        )

    for place in (7, 1, 6, 2, 5, 3, 4, 0):
        load_proj((z + place) % NZ).start()

    route = jnp.concatenate(
        [routes[0].astype(F32), jnp.zeros((N_DP, 128 - CAP), F32)], axis=1
    )
    route = jnp.concatenate([route, jnp.zeros((128 - N_DP, 128), F32)], axis=0).T
    row_number = lax.broadcasted_iota(jnp.int32, (CAP, ROWS), 1).astype(F32)
    for d in range(N_DP):
        hit = jnp.broadcast_to(route[0:CAP, d : d + 1], (CAP, ROWS)) == row_number
        onehot[d * CAP : (d + 1) * CAP, :] = jnp.where(hit, 1.0, 0.0).astype(BF)

    def to_slots(src, dst, cols=pl.ds(0, FEAT)):
        def one(b, carry):
            rows = pl.ds(aligned(b * 384, 384), 384)
            dst[rows, cols] = jnp.dot(
                onehot[rows, :], src[:, cols], preferred_element_type=F32
            ).astype(BF)
            return carry

        lax.fori_loop(0, 4, one, 0)

    def slot_rows(s):
        return pl.ds(aligned(s * CAP, 32), CAP)

    everything = pl.ds(0, FEAT)

    def a2a_copy(src, dst, sems, cols, d):
        peer = (dp + d) % N_DP
        return pltpu.make_async_remote_copy(
            src_ref=src.at[slot_rows(peer), cols],
            dst_ref=dst.at[slot_rows(dp), cols],
            send_sem=sems.at[0, d - 1],
            recv_sem=sems.at[1, d - 1],
            device_id=(peer, ten),
            device_id_type=MESH,
        )

    def each_peer(action):
        def one(d, carry):
            action(d)
            return carry

        lax.fori_loop(1, N_TEN, one, 0)

    def a2a_start(src, dst, sems, cols=everything):
        each_peer(lambda d: a2a_copy(src, dst, sems, cols, d).start())
        dst[slot_rows(dp), cols] = src[slot_rows(dp), cols]

    def a2a_wait(src, dst, sems, cols=everything):
        each_peer(lambda d: a2a_copy(src, dst, sems, cols, d).wait())

    def stream_rows(i):
        return pl.ds(aligned(i * 128, 128), 128)

    def sign(i):
        return 1 - 2 * (i // 2)

    def part_cols(p):
        return pl.ds(*PHASES[p])

    def ring_copy(p, s, i):
        here = first.at[i] if s == 0 else ring.at[s - 1, i]
        peer = ((z + sign(i) + NZ) % NZ) * 2 + y
        return pltpu.make_async_remote_copy(
            src_ref=here.at[:, :, part_cols(p)],
            dst_ref=ring.at[s, i, :, :, part_cols(p)],
            send_sem=ring_sem.at[0, p, s, i],
            recv_sem=ring_sem.at[1, p, s, i],
            device_id=(dp, peer),
            device_id_type=MESH,
        )

    def partials(p, s):
        if p == 0 and s == 0:
            load_proj((z + 7) % NZ).wait()
            load_proj((z + 1) % NZ).wait()
        elif p == 0 and s < 3:
            load_proj((z + 7 - s) % NZ).wait()
            load_proj((z + 1 + s) % NZ).wait()
        elif p == 0 and s == 3:
            load_proj((z + 4) % NZ).wait()
        elif p == 0 and s == 7:
            load_proj(z).wait()
        start, width = PHASES[p]

        def one(way, carry):
            c = (z + 2 * NZ - (1 - 2 * way) * (s + 1)) % NZ
            rows = pl.ds(aligned(way * 256, 256), 256)
            for j in range(2):
                cols = pl.ds(aligned(c * 1024 + j * 512 + start, 128), width)
                part[way, j, :, part_cols(p)] = jnp.dot(
                    tok[rows, :], proj_v[:, cols], preferred_element_type=F32
                )
            return carry

        lax.fori_loop(0, 2, one, 0)

    def my_part(p, i, j):
        rows = pl.ds(aligned((i % 2) * 128, 128), 128)
        return part[i // 2, j, rows, part_cols(p)]

    def each_stream(action):
        def one(k, carry):
            action((k % 2) * 2 + k // 2)
            return carry

        lax.fori_loop(0, 4, one, 0)

    def first_sends(p):
        def one(i):
            for j in range(2):
                first[i, j, :, part_cols(p)] = my_part(p, i, j).astype(BF)
            ring_copy(p, 0, i).start()

        each_stream(one)
        partials(p, 1)

    def ring_step(p, s):
        def one(i):
            ring_copy(p, s - 1, i).wait_recv()
            for j in range(2):
                ring[s - 1, i, j, :, part_cols(p)] = (
                    my_part(p, i, j) + ring[s - 1, i, j, :, part_cols(p)].astype(F32)
                ).astype(BF)
            ring_copy(p, s, i).start()

        each_stream(one)
        partials(p, s + 1)

    def y_copy(p, i):
        return pltpu.make_async_remote_copy(
            src_ref=ysend.at[i, :, part_cols(p)],
            dst_ref=yrecv.at[i, :, part_cols(p)],
            send_sem=y_sem.at[0, p, i],
            recv_sem=y_sem.at[1, p, i],
            device_id=(dp, z * 2 + 1 - y),
            device_id_type=MESH,
        )

    def last_hop(p):
        cols = part_cols(p)

        def one(i):
            ring_copy(p, NZ - 2, i).wait_recv()
            ysend[i, :, cols] = (
                my_part(p, i, 1 - y) + ring[NZ - 2, i, 1 - y, :, cols].astype(F32)
            ).astype(BF)
            y_copy(p, i).start()
            hidden[stream_rows(i), cols] = my_part(p, i, y) + ring[
                NZ - 2, i, y, :, cols
            ].astype(F32)

        each_stream(one)

    def y_finish(p):
        cols = part_cols(p)

        def one(i, carry):
            y_copy(p, i).wait()
            rows = stream_rows(i)
            total = hidden[rows, cols] + yrecv[i, :, cols].astype(F32)
            hidden[rows, cols] = total
            h_rows[rows, cols] = total.astype(BF)
            return carry

        lax.fori_loop(0, 4, one, 0)

    def to_owners(p):
        to_slots(h_rows, h_out, part_cols(p))
        a2a_start(h_out, h_slots, h_sem.at[p], part_cols(p))

    def chunk(arr, t, g, n):
        wide = LANES // n
        return arr.at[
            pl.ds(aligned((t // 4) * 16, 16), 16),
            pl.ds(aligned(g * 4 * wide + (t % 4) * wide, 128), wide),
        ]

    def landed(land, d, g, n):
        return land.at[d, :, pl.ds(g * (LANES // n), LANES // n)]

    def scatter_copy(part, land, g, n, d):
        peer = (ten + d) % N_TEN
        return pltpu.make_async_remote_copy(
            src_ref=chunk(part, peer, g, n),
            dst_ref=landed(land, d - 1, g, n),
            send_sem=ar_sem.at[n - 1 + g, 0, d - 1],
            recv_sem=ar_sem.at[n - 1 + g, 1, d - 1],
            device_id=(dp, peer),
            device_id_type=MESH,
        )

    def spread_copy(full, g, n, d):
        return pltpu.make_async_remote_copy(
            src_ref=chunk(full, ten, g, n),
            dst_ref=chunk(full, ten, g, n),
            send_sem=ar_sem.at[n - 1 + g, 2, d - 1],
            recv_sem=ar_sem.at[n - 1 + g, 3, d - 1],
            device_id=(dp, (ten + d) % N_TEN),
            device_id_type=MESH,
        )

    def ar_first(part, land, g, n):
        each_peer(lambda d: scatter_copy(part, land, g, n, d).start())

    def ar_second(part, land, full, g, n):
        each_peer(lambda d: scatter_copy(part, land, g, n, d).wait())
        total = chunk(part, ten, g, n)[...].astype(F32)
        for d in range(N_TEN - 1):
            total = total + landed(land, d, g, n)[...].astype(F32)
        chunk(full, ten, g, n)[...] = total.astype(BF)
        each_peer(lambda d: spread_copy(full, g, n, d).start())

    def ar_wait(full, g, n):
        each_peer(lambda d: spread_copy(full, g, n, d).wait())

    def low_rank(weights, rows_ref, scale, out, tiles=(0, SLOTS // 256)):
        def one(j, carry):
            lanes = pl.ds(aligned(j * 256, 256), 256)
            full = lax.dot_general(
                weights[...], rows_ref[lanes, :], NT, preferred_element_type=F32
            )
            tenant = jnp.broadcast_to(trow[:, lanes], (RANK, 256))
            total = jnp.zeros((RANK, 256), F32)
            for t in range(TEN):
                total = total + jnp.where(
                    tenant == t + 1.0, full[t * RANK : (t + 1) * RANK, :], 0.0
                )
            out[:, lanes] = (scale * total).astype(BF)
            return carry

        lax.fori_loop(*tiles, one, 0)

    def spread_tenants(full, tiles=(0, SLOTS // 256)):
        def one(j, carry):
            lanes = pl.ds(aligned(j * 256, 256), 256)
            value = full[:, lanes].astype(F32)
            tenant = jnp.broadcast_to(trow[:, lanes], (RANK, 256))
            for t in range(TEN):
                expand_t[t * RANK : (t + 1) * RANK, lanes] = jnp.where(
                    tenant == t + 1.0, value, 0.0
                ).astype(BF)
            return carry

        lax.fori_loop(*tiles, one, 0)

    def grouped_outer(rows_ref, scale, out):
        def one(t, carry):
            rows = pl.ds(aligned(t * 256, 256), 256)
            out[rows, :] = (
                scale
                * jnp.dot(expand_t[rows, :], rows_ref[...], preferred_element_type=F32)
            ).astype(BF)
            return carry

        lax.fori_loop(0, TEN * RANK // 256, one, 0)

    def slot_tenants():
        held = positions[...]
        count = held.shape[1]
        owner = jnp.concatenate(
            [
                jnp.broadcast_to(blocks[:, b : b + 1].astype(F32) + 1.0, (1, 128))
                for b in range(count // 128)
            ],
            axis=1,
        )
        high = jnp.where(
            jnp.broadcast_to(held // 128, (16, count))
            == lax.broadcasted_iota(jnp.int32, (16, count), 0),
            1.0,
            0.0,
        ).astype(BF)
        low = jnp.where(
            jnp.broadcast_to(held % 128, (128, count))
            == lax.broadcasted_iota(jnp.int32, (128, count), 0),
            jnp.broadcast_to(owner, (128, count)),
            0.0,
        ).astype(BF)
        table = lax.dot_general(high, low, NT, preferred_element_type=F32)
        columns = jnp.concatenate([table, jnp.zeros((112, 128), F32)], axis=0).T
        for a in range(SLOTS // 128):
            trow[:, a * 128 : (a + 1) * 128] = table[a : a + 1, :]
            tcol[a * 128 : (a + 1) * 128, :] = jnp.broadcast_to(
                columns[:, a : a + 1], (128, 128)
            )

    def deltas(b, carry):
        rows = pl.ds(aligned(b * 256, 256), 256)
        value = rank_full[:, rows].astype(F32)
        twice = jnp.concatenate([value, value], axis=0).T
        lane = lax.broadcasted_iota(jnp.int32, (256, 128), 1)
        tenant = tcol[rows, :] - jnp.where(lane >= RANK, 1.0, 0.0)
        for j in range(TEN // 2):
            expand[:, j * 128 : (j + 1) * 128] = jnp.where(
                tenant == 2.0 * j + 1.0, twice, 0.0
            ).astype(BF)
        delta_out[rows, :] = (
            2.0 * jnp.dot(expand[...], up[...], preferred_element_type=F32)
        ).astype(BF)
        return carry

    def scatter_rows():
        for q in range(4):
            cols = pl.ds(q * 128, 128)
            delta_rows[cols, :] = lax.dot_general(
                onehot[:, cols], back_slots[...], TN, preferred_element_type=F32
            )

    def stats(p, i):
        rows, cols = pl.ds(i * 128, 128), part_cols(p)
        h = hidden[rows, cols] + delta_rows[rows, cols]
        hidden[rows, cols] = h
        gh = gain[:, cols] * h
        s1 = jnp.sum(h * h, axis=1, keepdims=True)
        s2 = jnp.sum(gh * gh, axis=1, keepdims=True)
        s3 = jnp.sum(gh * target[rows, cols].astype(F32), axis=1, keepdims=True)
        lane = lax.broadcasted_iota(jnp.int32, (128, 128), 1)
        return jnp.where(lane == 0, s1, jnp.where(lane == 1, s2, s3))

    def early_stats():
        for i in range(4):
            stat_acc[i] = stats(0, i)

    to_slots(tok, tok_out)
    partials(0, 0)
    pl.semaphore_wait(barrier, 2 * (N_DP - 1))
    a2a_start(tok_out, feat, a2a_sem.at[0])
    first_sends(0)
    scal_send[...] = jnp.zeros_like(scal_send)
    slot_tenants()
    to_slots(target, tgt_out)
    a2a_start(tgt_out, tgt_slots, a2a_sem.at[2])
    ring_step(0, 1)
    ring_step(0, 2)
    a2a_wait(tok_out, feat, a2a_sem.at[0])
    low_rank(down, feat, 1.0, rank_part)
    ar_first(rank_part, rank_land, 0, 1)
    ring_step(0, 3)
    ar_second(rank_part, rank_land, rank_full, 0, 1)
    ring_step(0, 4)
    ar_wait(rank_full, 0, 1)
    lax.fori_loop(0, SLOTS // 256, deltas, 0)
    a2a_start(delta_out, back_slots, a2a_sem.at[1])
    ring_step(0, 5)
    partials(1, 0)
    first_sends(1)
    ring_step(0, 6)
    ring_step(1, 1)
    last_hop(0)
    ring_step(1, 2)
    ring_step(1, 3)
    y_finish(0)
    to_owners(0)
    ring_step(1, 4)
    ring_step(1, 5)
    a2a_wait(delta_out, back_slots, a2a_sem.at[1])
    scatter_rows()
    early_stats()
    ring_step(1, 6)
    spread_tenants(rank_full)
    last_hop(1)
    y_finish(1)

    for i in range(4):
        table = stat_acc[i] + stats(1, i)
        stat_send[4 * i : 4 * i + 4, :] = table.T[0:4, :]

    def stat_copy(d):
        return pltpu.make_async_remote_copy(
            src_ref=stat_send,
            dst_ref=stat_land.at[d - 1],
            send_sem=stat_sem.at[0, d - 1],
            recv_sem=stat_sem.at[1, d - 1],
            device_id=(dp, (ten + d) % N_TEN),
            device_id_type=MESH,
        )

    each_peer(lambda d: stat_copy(d).start())
    to_owners(1)
    each_peer(lambda d: stat_copy(d).wait())

    total = stat_send[...]
    for d in range(N_TEN - 1):
        total = total + stat_land[d]
    invs, dots = [], []
    for i in range(4):
        s1, s2, s3 = (total[4 * i + q : 4 * i + q + 1, :] for q in range(3))
        inv = lax.rsqrt(s1 / MODEL_WIDTH + 1e-05)
        invs.append(inv)
        dots.append(inv * (inv * s2 - s3) / (8.0 * MODEL_WIDTH))

    pieces = []
    for rest in (jnp.concatenate(invs, axis=1), jnp.concatenate(dots, axis=1)):
        for _ in range(3):
            piece = rest.astype(BF).astype(F32)
            pieces.append(piece)
            rest = rest - piece
    pieces.append(jnp.zeros((10, ROWS), F32))
    placed = lax.dot_general(
        jnp.concatenate(pieces, axis=0).astype(BF),
        onehot[...],
        NT,
        preferred_element_type=F32,
    )
    pair = jnp.concatenate(
        [
            placed[0:1] + placed[1:2] + placed[2:3],
            placed[3:4] + placed[4:5] + placed[5:6],
        ],
        axis=0,
    )
    for d in range(N_DP):
        scal_send[d, 0:2, 0:CAP] = pair[:, d * CAP : (d + 1) * CAP]

    def scal_copy(d):
        peer = (dp + d) % N_DP
        return pltpu.make_async_remote_copy(
            src_ref=scal_send.at[peer],
            dst_ref=scal_land.at[dp],
            send_sem=scal_sem.at[0, d - 1],
            recv_sem=scal_sem.at[1, d - 1],
            device_id=(peer, ten),
            device_id_type=MESH,
        )

    each_peer(lambda d: scal_copy(d).start())
    scal_land[dp] = scal_send[dp]

    for i in range(4):
        rows = pl.ds(i * 128, 128)
        table = jnp.concatenate([invs[i], jnp.zeros((127, 128), F32)], axis=0).T
        inv = table[:, 0:1]
        draft[rows, :] = (hidden[rows, :] * inv * gain[...]).astype(BF)

    a2a_wait(tgt_out, tgt_slots, a2a_sem.at[2])
    for p in range(len(PHASES)):
        a2a_wait(h_out, h_slots, h_sem.at[p], part_cols(p))
    each_peer(lambda d: scal_copy(d).wait())

    def grads(s, carry):
        rows = slot_rows(s)
        table = jnp.concatenate([scal_land[s], jnp.zeros((120, 128), F32)], axis=0).T
        inv, dot = table[0:CAP, 0:1], table[0:CAP, 1:2]
        g = gain[...]
        h = h_slots[rows, :].astype(F32) + delta_out[rows, :].astype(F32)
        scaled = h * inv
        weighted = g * ((scaled * g - tgt_slots[rows, :].astype(F32)) / 8.0)
        gslots[rows, :] = (inv * (weighted - scaled * dot)).astype(BF)
        return carry

    for g, sources in enumerate(((0, 6), (6, 11), (11, N_DP))):
        lax.fori_loop(*sources, grads, 0)
        low_rank(up, gslots, 2.0, back_part, (2 * g, 2 * g + 2))
        ar_first(back_part, back_land, g, 3)
    for g in range(3):
        ar_second(back_part, back_land, back_full, g, 3)
    grouped_outer(gslots, 2.0, gup)
    for g in range(3):
        ar_wait(back_full, g, 3)
        spread_tenants(back_full, (2 * g, 2 * g + 2))
    grouped_outer(feat, 1.0, gdown)

    for p in range(len(PHASES)):
        for s in range(NZ - 1):

            def drain(i, carry, p=p, s=s):
                ring_copy(p, s, i).wait_send()
                return carry

            lax.fori_loop(0, 4, drain, 0)


def body(
    tokens,
    proj,
    gain,
    target,
    adapter_down_weight,
    adapter_up_weight,
    source_row_index,
    padded_row_index,
    padded_block_tenant,
):
    vmem = pl.BlockSpec(memory_space=pltpu.VMEM)
    wide = TEN * RANK
    dma = pltpu.SemaphoreType.DMA
    draft, grad_down, grad_up = pl.pallas_call(
        kernel,
        out_shape=(
            jax.ShapeDtypeStruct((ROWS, FEAT), BF),
            jax.ShapeDtypeStruct((wide, FEAT), BF),
            jax.ShapeDtypeStruct((wide, FEAT), BF),
        ),
        in_specs=[vmem, pl.BlockSpec(memory_space=pl.ANY)] + [vmem] * 7,
        out_specs=(vmem, vmem, vmem),
        scratch_shapes=[
            pltpu.VMEM((FEAT, MODEL_WIDTH), BF),
            pltpu.VMEM((SLOTS, ROWS), BF),
            pltpu.VMEM((SLOTS, FEAT), BF),
            pltpu.VMEM((SLOTS, FEAT), BF),
            pltpu.VMEM((SLOTS, FEAT), BF),
            pltpu.VMEM((SLOTS, FEAT), BF),
            pltpu.VMEM((SLOTS, FEAT), BF),
            pltpu.VMEM((SLOTS, FEAT), BF),
            pltpu.VMEM((SLOTS, FEAT), BF),
            pltpu.VMEM((SLOTS, FEAT), BF),
            pltpu.VMEM((SLOTS, FEAT), BF),
            pltpu.VMEM((256, wide), BF),
            pltpu.VMEM((wide, SLOTS), BF),
            pltpu.VMEM((2, 2, 256, FEAT), F32),
            pltpu.VMEM((4, 2, 128, FEAT), BF),
            pltpu.VMEM((NZ - 1, 4, 2, 128, FEAT), BF),
            pltpu.VMEM((4, 128, FEAT), BF),
            pltpu.VMEM((4, 128, FEAT), BF),
            pltpu.VMEM((ROWS, FEAT), F32),
            pltpu.VMEM((ROWS, FEAT), F32),
            pltpu.VMEM((ROWS, FEAT), BF),
            pltpu.VMEM((RANK, SLOTS), BF),
            pltpu.VMEM((N_TEN - 1, 16, LANES), BF),
            pltpu.VMEM((RANK, SLOTS), BF),
            pltpu.VMEM((RANK, SLOTS), BF),
            pltpu.VMEM((N_TEN - 1, 16, LANES), BF),
            pltpu.VMEM((RANK, SLOTS), BF),
            pltpu.VMEM((1, SLOTS), F32),
            pltpu.VMEM((SLOTS, 128), F32),
            pltpu.VMEM((4, 128, 128), F32),
            pltpu.VMEM((16, 128), F32),
            pltpu.VMEM((N_TEN - 1, 16, 128), F32),
            pltpu.VMEM((N_DP, 8, 128), F32),
            pltpu.VMEM((N_DP, 8, 128), F32),
            dma((NZ,)),
            dma((3, 2, N_DP - 1)),
            dma((len(PHASES), 2, N_DP - 1)),
            dma((2, N_DP - 1)),
            dma((2, len(PHASES), NZ - 1, 4)),
            dma((5, 4, N_TEN - 1)),
            dma((2, len(PHASES), 4)),
            dma((2, N_TEN - 1)),
        ],
        compiler_params=pltpu.CompilerParams(
            collective_id=0, has_side_effects=True, vmem_limit_bytes=58 << 20
        ),
        name="step",
    )(
        tokens,
        proj,
        gain.reshape(1, FEAT),
        target,
        adapter_down_weight.reshape(wide, FEAT),
        adapter_up_weight.reshape(wide, FEAT),
        source_row_index,
        padded_row_index,
        padded_block_tenant,
    )
    return (
        draft,
        grad_down.reshape(TEN, RANK, FEAT),
        grad_up.reshape(TEN, RANK, FEAT),
    )


def solution(mesh):
    return jax.shard_map(
        body,
        mesh=mesh,
        in_specs=(
            P("dp", "tensor"),
            P("tensor", None),
            P("tensor"),
            P("dp", "tensor"),
            P("dp", None, "tensor"),
            P("dp", None, "tensor"),
            P("dp", None, None),
            P("dp", None),
            P("dp", None),
        ),
        out_specs=(P("dp", "tensor"), P("dp", None, "tensor"), P("dp", None, "tensor")),
        check_vma=False,
    )
```

```python
import jax
import jax.numpy as jnp
from jax import lax
from jax.experimental import pallas as pl
from jax.experimental.pallas import tpu as pltpu
from jax.sharding import PartitionSpec as P

MODEL_WIDTH = 8192
MESH = pl.DeviceIdType.MESH
BF = jnp.bfloat16
F32 = jnp.float32
NT = (((1,), (1,)), ((), ()))
TN = (((0,), (0,)), ((), ()))

N_DP = 16
N_TEN = 16
NZ = 8
CAP = 96
SLOTS = N_DP * CAP
TEN = 16
RANK = 64
ROWS = 512
FEAT = 512
LANES = SLOTS // 4
PHASES = ((0, 384), (384, 128))


def aligned(value, multiple):
    return pl.multiple_of(value, multiple)


def kernel(
    tok, proj, gain, target, down, up, routes, positions, blocks,
    draft_out, gdown_out, gup_out,
    draft, gdown, gup, proj_v, onehot, tok_out, tgt_out, delta_out, h_out, feat, tgt_slots,
    back_slots, h_slots, gslots, expand, expand_t,
    part, first, ring, ysend, yrecv, hidden, delta_rows, h_rows,
    rank_part, rank_land, rank_full, back_part, back_land, back_full,
    trow, tcol, stat_acc, stat_send, stat_land, scal_send, scal_land,
    out_sem, proj_sem, a2a_sem, h_sem, scal_sem, ring_sem, ar_sem, y_sem, stat_sem,
):
    dp = lax.axis_index("dp")
    ten = lax.axis_index("tensor")
    z, y = ten // 2, ten % 2

    barrier = pltpu.get_barrier_semaphore()

    def greet(d, carry):
        pl.semaphore_signal(
            barrier, inc=1, device_id=((dp + d) % N_DP, ten), device_id_type=MESH
        )
        pl.semaphore_signal(
            barrier, inc=1, device_id=(dp, (ten + d) % N_TEN), device_id_type=MESH
        )
        return carry

    lax.fori_loop(1, N_DP, greet, 0)

    def chunk_cols(c):
        return pl.ds(aligned(c * 1024, 1024), 1024)

    def load_proj(c):
        return pltpu.make_async_copy(
            proj.at[:, chunk_cols(c)], proj_v.at[:, chunk_cols(c)], proj_sem.at[c]
        )

    for place in (7, 1, 6, 2, 5, 3, 4, 0):
        load_proj((z + place) % NZ).start()

    route = jnp.concatenate(
        [routes[0].astype(F32), jnp.zeros((N_DP, 128 - CAP), F32)], axis=1
    )
    route = jnp.concatenate([route, jnp.zeros((128 - N_DP, 128), F32)], axis=0).T
    row_number = lax.broadcasted_iota(jnp.int32, (CAP, ROWS), 1).astype(F32)
    for d in range(N_DP):
        hit = jnp.broadcast_to(route[0:CAP, d : d + 1], (CAP, ROWS)) == row_number
        onehot[d * CAP : (d + 1) * CAP, :] = jnp.where(hit, 1.0, 0.0).astype(BF)

    def to_slots(src, dst, cols=pl.ds(0, FEAT)):
        def one(b, carry):
            rows = pl.ds(aligned(b * 384, 384), 384)
            dst[rows, cols] = jnp.dot(
                onehot[rows, :], src[:, cols], preferred_element_type=F32
            ).astype(BF)
            return carry

        lax.fori_loop(0, 4, one, 0)

    def slot_rows(s):
        return pl.ds(aligned(s * CAP, 32), CAP)

    everything = pl.ds(0, FEAT)

    def a2a_copy(src, dst, sems, cols, d):
        peer = (dp + d) % N_DP
        return pltpu.make_async_remote_copy(
            src_ref=src.at[slot_rows(peer), cols],
            dst_ref=dst.at[slot_rows(dp), cols],
            send_sem=sems.at[0, d - 1],
            recv_sem=sems.at[1, d - 1],
            device_id=(peer, ten),
            device_id_type=MESH,
        )

    def each_peer(action):
        def one(d, carry):
            action(d)
            return carry

        lax.fori_loop(1, N_TEN, one, 0)

    def a2a_start(src, dst, sems, cols=everything):
        each_peer(lambda d: a2a_copy(src, dst, sems, cols, d).start())
        dst[slot_rows(dp), cols] = src[slot_rows(dp), cols]

    def a2a_wait(src, dst, sems, cols=everything):
        each_peer(lambda d: a2a_copy(src, dst, sems, cols, d).wait())

    def stream_rows(i):
        return pl.ds(aligned(i * 128, 128), 128)

    def sign(i):
        return 1 - 2 * (i // 2)

    def part_cols(p):
        return pl.ds(*PHASES[p])

    def ring_copy(p, s, i):
        here = first.at[i] if s == 0 else ring.at[s - 1, i]
        peer = ((z + sign(i) + NZ) % NZ) * 2 + y
        return pltpu.make_async_remote_copy(
            src_ref=here.at[:, :, part_cols(p)],
            dst_ref=ring.at[s, i, :, :, part_cols(p)],
            send_sem=ring_sem.at[0, p, s, i],
            recv_sem=ring_sem.at[1, p, s, i],
            device_id=(dp, peer),
            device_id_type=MESH,
        )

    def partials(p, s):
        if p == 0 and s == 0:
            load_proj((z + 7) % NZ).wait()
            load_proj((z + 1) % NZ).wait()
        elif p == 0 and s < 3:
            load_proj((z + 7 - s) % NZ).wait()
            load_proj((z + 1 + s) % NZ).wait()
        elif p == 0 and s == 3:
            load_proj((z + 4) % NZ).wait()
        elif p == 0 and s == 7:
            load_proj(z).wait()
        start, width = PHASES[p]

        def one(way, carry):
            c = (z + 2 * NZ - (1 - 2 * way) * (s + 1)) % NZ
            rows = pl.ds(aligned(way * 256, 256), 256)
            for j in range(2):
                cols = pl.ds(aligned(c * 1024 + j * 512 + start, 128), width)
                part[way, j, :, part_cols(p)] = jnp.dot(
                    tok[rows, :], proj_v[:, cols], preferred_element_type=F32
                )
            return carry

        lax.fori_loop(0, 2, one, 0)

    def my_part(p, i, j):
        rows = pl.ds(aligned((i % 2) * 128, 128), 128)
        return part[i // 2, j, rows, part_cols(p)]

    def each_stream(action):
        def one(k, carry):
            action((k % 2) * 2 + k // 2)
            return carry

        lax.fori_loop(0, 4, one, 0)

    def first_sends(p):
        def one(i):
            for j in range(2):
                first[i, j, :, part_cols(p)] = my_part(p, i, j).astype(BF)
            ring_copy(p, 0, i).start()

        each_stream(one)
        partials(p, 1)

    def ring_step(p, s):
        def one(i):
            ring_copy(p, s - 1, i).wait_recv()
            for j in range(2):
                ring[s - 1, i, j, :, part_cols(p)] = (
                    my_part(p, i, j) + ring[s - 1, i, j, :, part_cols(p)].astype(F32)
                ).astype(BF)
            ring_copy(p, s, i).start()

        each_stream(one)
        partials(p, s + 1)

    def y_copy(p, i):
        return pltpu.make_async_remote_copy(
            src_ref=ysend.at[i, :, part_cols(p)],
            dst_ref=yrecv.at[i, :, part_cols(p)],
            send_sem=y_sem.at[0, p, i],
            recv_sem=y_sem.at[1, p, i],
            device_id=(dp, z * 2 + 1 - y),
            device_id_type=MESH,
        )

    def last_hop(p):
        cols = part_cols(p)

        def one(i):
            ring_copy(p, NZ - 2, i).wait_recv()
            ysend[i, :, cols] = (
                my_part(p, i, 1 - y) + ring[NZ - 2, i, 1 - y, :, cols].astype(F32)
            ).astype(BF)
            y_copy(p, i).start()
            hidden[stream_rows(i), cols] = my_part(p, i, y) + ring[
                NZ - 2, i, y, :, cols
            ].astype(F32)

        each_stream(one)

    def y_finish(p):
        cols = part_cols(p)

        def one(i, carry):
            y_copy(p, i).wait()
            rows = stream_rows(i)
            total = hidden[rows, cols] + yrecv[i, :, cols].astype(F32)
            hidden[rows, cols] = total
            h_rows[rows, cols] = total.astype(BF)
            return carry

        lax.fori_loop(0, 4, one, 0)

    def to_owners(p):
        to_slots(h_rows, h_out, part_cols(p))
        a2a_start(h_out, h_slots, h_sem.at[p], part_cols(p))

    def chunk(arr, t, g, n):
        wide = LANES // n
        return arr.at[
            pl.ds(aligned((t // 4) * 16, 16), 16),
            pl.ds(aligned(g * 4 * wide + (t % 4) * wide, 128), wide),
        ]

    def landed(land, d, g, n):
        return land.at[d, :, pl.ds(g * (LANES // n), LANES // n)]

    def scatter_copy(part, land, g, n, d):
        peer = (ten + d) % N_TEN
        return pltpu.make_async_remote_copy(
            src_ref=chunk(part, peer, g, n),
            dst_ref=landed(land, d - 1, g, n),
            send_sem=ar_sem.at[n - 1 + g, 0, d - 1],
            recv_sem=ar_sem.at[n - 1 + g, 1, d - 1],
            device_id=(dp, peer),
            device_id_type=MESH,
        )

    def spread_copy(full, g, n, d):
        return pltpu.make_async_remote_copy(
            src_ref=chunk(full, ten, g, n),
            dst_ref=chunk(full, ten, g, n),
            send_sem=ar_sem.at[n - 1 + g, 2, d - 1],
            recv_sem=ar_sem.at[n - 1 + g, 3, d - 1],
            device_id=(dp, (ten + d) % N_TEN),
            device_id_type=MESH,
        )

    def ar_first(part, land, g, n):
        each_peer(lambda d: scatter_copy(part, land, g, n, d).start())

    def ar_second(part, land, full, g, n):
        each_peer(lambda d: scatter_copy(part, land, g, n, d).wait())
        total = chunk(part, ten, g, n)[...].astype(F32)
        for d in range(N_TEN - 1):
            total = total + landed(land, d, g, n)[...].astype(F32)
        chunk(full, ten, g, n)[...] = total.astype(BF)
        each_peer(lambda d: spread_copy(full, g, n, d).start())

    def ar_wait(full, g, n):
        each_peer(lambda d: spread_copy(full, g, n, d).wait())

    def low_rank(weights, rows_ref, scale, out, tiles=(0, SLOTS // 256)):
        def one(j, carry):
            lanes = pl.ds(aligned(j * 256, 256), 256)
            full = lax.dot_general(
                weights[...], rows_ref[lanes, :], NT, preferred_element_type=F32
            )
            tenant = jnp.broadcast_to(trow[:, lanes], (RANK, 256))
            total = jnp.zeros((RANK, 256), F32)
            for t in range(TEN):
                total = total + jnp.where(
                    tenant == t + 1.0, full[t * RANK : (t + 1) * RANK, :], 0.0
                )
            out[:, lanes] = (scale * total).astype(BF)
            return carry

        lax.fori_loop(*tiles, one, 0)

    def spread_tenants(full, tiles=(0, SLOTS // 256)):
        def one(j, carry):
            lanes = pl.ds(aligned(j * 256, 256), 256)
            value = full[:, lanes].astype(F32)
            tenant = jnp.broadcast_to(trow[:, lanes], (RANK, 256))
            for t in range(TEN):
                expand_t[t * RANK : (t + 1) * RANK, lanes] = jnp.where(
                    tenant == t + 1.0, value, 0.0
                ).astype(BF)
            return carry

        lax.fori_loop(*tiles, one, 0)

    def grouped_outer(rows_ref, scale, out, after=None):
        def one(t, carry):
            rows = pl.ds(aligned(t * 256, 256), 256)
            out[rows, :] = (
                scale
                * jnp.dot(expand_t[rows, :], rows_ref[...], preferred_element_type=F32)
            ).astype(BF)
            if after:
                after(t).start()
            return carry

        lax.fori_loop(0, TEN * RANK // 256, one, 0)

    def slot_tenants():
        held = positions[...]
        count = held.shape[1]
        owner = jnp.concatenate(
            [
                jnp.broadcast_to(blocks[:, b : b + 1].astype(F32) + 1.0, (1, 128))
                for b in range(count // 128)
            ],
            axis=1,
        )
        high = jnp.where(
            jnp.broadcast_to(held // 128, (16, count))
            == lax.broadcasted_iota(jnp.int32, (16, count), 0),
            1.0,
            0.0,
        ).astype(BF)
        low = jnp.where(
            jnp.broadcast_to(held % 128, (128, count))
            == lax.broadcasted_iota(jnp.int32, (128, count), 0),
            jnp.broadcast_to(owner, (128, count)),
            0.0,
        ).astype(BF)
        table = lax.dot_general(high, low, NT, preferred_element_type=F32)
        columns = jnp.concatenate([table, jnp.zeros((112, 128), F32)], axis=0).T
        for a in range(SLOTS // 128):
            trow[:, a * 128 : (a + 1) * 128] = table[a : a + 1, :]
            tcol[a * 128 : (a + 1) * 128, :] = jnp.broadcast_to(
                columns[:, a : a + 1], (128, 128)
            )

    def deltas(b, carry):
        rows = pl.ds(aligned(b * 256, 256), 256)
        value = rank_full[:, rows].astype(F32)
        twice = jnp.concatenate([value, value], axis=0).T
        lane = lax.broadcasted_iota(jnp.int32, (256, 128), 1)
        tenant = tcol[rows, :] - jnp.where(lane >= RANK, 1.0, 0.0)
        for j in range(TEN // 2):
            expand[:, j * 128 : (j + 1) * 128] = jnp.where(
                tenant == 2.0 * j + 1.0, twice, 0.0
            ).astype(BF)
        delta_out[rows, :] = (
            2.0 * jnp.dot(expand[...], up[...], preferred_element_type=F32)
        ).astype(BF)
        return carry

    def scatter_rows():
        for q in range(4):
            cols = pl.ds(q * 128, 128)
            delta_rows[cols, :] = lax.dot_general(
                onehot[:, cols], back_slots[...], TN, preferred_element_type=F32
            )

    def stats(p, i):
        rows, cols = pl.ds(i * 128, 128), part_cols(p)
        h = hidden[rows, cols] + delta_rows[rows, cols]
        hidden[rows, cols] = h
        gh = gain[:, cols] * h
        s1 = jnp.sum(h * h, axis=1, keepdims=True)
        s2 = jnp.sum(gh * gh, axis=1, keepdims=True)
        s3 = jnp.sum(gh * target[rows, cols].astype(F32), axis=1, keepdims=True)
        lane = lax.broadcasted_iota(jnp.int32, (128, 128), 1)
        return jnp.where(lane == 0, s1, jnp.where(lane == 1, s2, s3))

    def early_stats():
        for i in range(4):
            stat_acc[i] = stats(0, i)

    to_slots(tok, tok_out)
    partials(0, 0)
    pl.semaphore_wait(barrier, 2 * (N_DP - 1))
    a2a_start(tok_out, feat, a2a_sem.at[0])
    first_sends(0)
    scal_send[...] = jnp.zeros_like(scal_send)
    slot_tenants()
    to_slots(target, tgt_out)
    a2a_start(tgt_out, tgt_slots, a2a_sem.at[2])
    ring_step(0, 1)
    ring_step(0, 2)
    a2a_wait(tok_out, feat, a2a_sem.at[0])
    low_rank(down, feat, 1.0, rank_part)
    ar_first(rank_part, rank_land, 0, 1)
    ring_step(0, 3)
    ar_second(rank_part, rank_land, rank_full, 0, 1)
    ring_step(0, 4)
    ar_wait(rank_full, 0, 1)
    lax.fori_loop(0, SLOTS // 256, deltas, 0)
    a2a_start(delta_out, back_slots, a2a_sem.at[1])
    ring_step(0, 5)
    partials(1, 0)
    first_sends(1)
    ring_step(0, 6)
    ring_step(1, 1)
    last_hop(0)
    ring_step(1, 2)
    ring_step(1, 3)
    y_finish(0)
    to_owners(0)
    ring_step(1, 4)
    ring_step(1, 5)
    a2a_wait(delta_out, back_slots, a2a_sem.at[1])
    scatter_rows()
    early_stats()
    ring_step(1, 6)
    spread_tenants(rank_full)
    last_hop(1)
    y_finish(1)

    for i in range(4):
        table = stat_acc[i] + stats(1, i)
        stat_send[4 * i : 4 * i + 4, :] = table.T[0:4, :]

    def stat_copy(d):
        return pltpu.make_async_remote_copy(
            src_ref=stat_send,
            dst_ref=stat_land.at[d - 1],
            send_sem=stat_sem.at[0, d - 1],
            recv_sem=stat_sem.at[1, d - 1],
            device_id=(dp, (ten + d) % N_TEN),
            device_id_type=MESH,
        )

    each_peer(lambda d: stat_copy(d).start())
    to_owners(1)
    each_peer(lambda d: stat_copy(d).wait())

    total = stat_send[...]
    for d in range(N_TEN - 1):
        total = total + stat_land[d]
    invs, dots = [], []
    for i in range(4):
        s1, s2, s3 = (total[4 * i + q : 4 * i + q + 1, :] for q in range(3))
        inv = lax.rsqrt(s1 / MODEL_WIDTH + 1e-05)
        invs.append(inv)
        dots.append(inv * (inv * s2 - s3) / (8.0 * MODEL_WIDTH))

    pieces = []
    for rest in (jnp.concatenate(invs, axis=1), jnp.concatenate(dots, axis=1)):
        for _ in range(3):
            piece = rest.astype(BF).astype(F32)
            pieces.append(piece)
            rest = rest - piece
    pieces.append(jnp.zeros((10, ROWS), F32))
    placed = lax.dot_general(
        jnp.concatenate(pieces, axis=0).astype(BF),
        onehot[...],
        NT,
        preferred_element_type=F32,
    )
    pair = jnp.concatenate(
        [
            placed[0:1] + placed[1:2] + placed[2:3],
            placed[3:4] + placed[4:5] + placed[5:6],
        ],
        axis=0,
    )
    for d in range(N_DP):
        scal_send[d, 0:2, 0:CAP] = pair[:, d * CAP : (d + 1) * CAP]

    def scal_copy(d):
        peer = (dp + d) % N_DP
        return pltpu.make_async_remote_copy(
            src_ref=scal_send.at[peer],
            dst_ref=scal_land.at[dp],
            send_sem=scal_sem.at[0, d - 1],
            recv_sem=scal_sem.at[1, d - 1],
            device_id=(peer, ten),
            device_id_type=MESH,
        )

    each_peer(lambda d: scal_copy(d).start())
    scal_land[dp] = scal_send[dp]

    for i in range(4):
        rows = pl.ds(i * 128, 128)
        table = jnp.concatenate([invs[i], jnp.zeros((127, 128), F32)], axis=0).T
        inv = table[:, 0:1]
        draft[rows, :] = (hidden[rows, :] * inv * gain[...]).astype(BF)
    store_draft = pltpu.make_async_copy(draft, draft_out, out_sem.at[0])
    store_draft.start()

    a2a_wait(tgt_out, tgt_slots, a2a_sem.at[2])
    for p in range(len(PHASES)):
        a2a_wait(h_out, h_slots, h_sem.at[p], part_cols(p))
    each_peer(lambda d: scal_copy(d).wait())

    def grads(s, carry):
        rows = slot_rows(s)
        table = jnp.concatenate([scal_land[s], jnp.zeros((120, 128), F32)], axis=0).T
        inv, dot = table[0:CAP, 0:1], table[0:CAP, 1:2]
        g = gain[...]
        h = h_slots[rows, :].astype(F32) + delta_out[rows, :].astype(F32)
        scaled = h * inv
        weighted = g * ((scaled * g - tgt_slots[rows, :].astype(F32)) / 8.0)
        gslots[rows, :] = (inv * (weighted - scaled * dot)).astype(BF)
        return carry

    for g, sources in enumerate(((0, 6), (6, 11), (11, N_DP))):
        lax.fori_loop(*sources, grads, 0)
        low_rank(up, gslots, 2.0, back_part, (2 * g, 2 * g + 2))
        ar_first(back_part, back_land, g, 3)
    for g in range(3):
        ar_second(back_part, back_land, back_full, g, 3)
    grouped_outer(gslots, 2.0, gup)
    store_up = pltpu.make_async_copy(gup, gup_out, out_sem.at[1])
    store_up.start()
    for g in range(3):
        ar_wait(back_full, g, 3)
        spread_tenants(back_full, (2 * g, 2 * g + 2))

    def store_down(t):
        rows = pl.ds(aligned(t * 256, 256), 256)
        return pltpu.make_async_copy(
            gdown.at[rows, :], gdown_out.at[rows, :], out_sem.at[2 + t]
        )

    grouped_outer(feat, 1.0, gdown, store_down)

    for p in range(len(PHASES)):
        for s in range(NZ - 1):

            def drain(i, carry, p=p, s=s):
                ring_copy(p, s, i).wait_send()
                return carry

            lax.fori_loop(0, 4, drain, 0)

    store_draft.wait()
    store_up.wait()
    for t in range(4):
        store_down(t).wait()


def hand_on(*refs):
    sems = refs[-1]
    copies = []
    for k in range(3):
        src, dst = refs[k], refs[3 + k]
        size = src.shape[0] // 4
        for q in range(4):
            rows = pl.ds(q * size, size)
            copies.append(
                pltpu.make_async_copy(
                    src.at[rows, :], dst.at[rows, :], sems.at[4 * k + q]
                )
            )
    for copy in copies:
        copy.start()
    for copy in copies:
        copy.wait()


def body(
    tokens,
    proj,
    gain,
    target,
    adapter_down_weight,
    adapter_up_weight,
    source_row_index,
    padded_row_index,
    padded_block_tenant,
):
    vmem = pl.BlockSpec(memory_space=pltpu.VMEM)
    hbm = pl.BlockSpec(memory_space=pl.ANY)
    wide = TEN * RANK
    dma = pltpu.SemaphoreType.DMA
    results = (
        jax.ShapeDtypeStruct((ROWS, FEAT), BF),
        jax.ShapeDtypeStruct((wide, FEAT), BF),
        jax.ShapeDtypeStruct((wide, FEAT), BF),
    )
    made = pl.pallas_call(
        kernel,
        out_shape=results,
        in_specs=[vmem, hbm] + [vmem] * 7,
        out_specs=(hbm, hbm, hbm),
        scratch_shapes=[
            pltpu.VMEM((ROWS, FEAT), BF),
            pltpu.VMEM((wide, FEAT), BF),
            pltpu.VMEM((wide, FEAT), BF),
            pltpu.VMEM((FEAT, MODEL_WIDTH), BF),
            pltpu.VMEM((SLOTS, ROWS), BF),
            pltpu.VMEM((SLOTS, FEAT), BF),
            pltpu.VMEM((SLOTS, FEAT), BF),
            pltpu.VMEM((SLOTS, FEAT), BF),
            pltpu.VMEM((SLOTS, FEAT), BF),
            pltpu.VMEM((SLOTS, FEAT), BF),
            pltpu.VMEM((SLOTS, FEAT), BF),
            pltpu.VMEM((SLOTS, FEAT), BF),
            pltpu.VMEM((SLOTS, FEAT), BF),
            pltpu.VMEM((SLOTS, FEAT), BF),
            pltpu.VMEM((256, wide), BF),
            pltpu.VMEM((wide, SLOTS), BF),
            pltpu.VMEM((2, 2, 256, FEAT), F32),
            pltpu.VMEM((4, 2, 128, FEAT), BF),
            pltpu.VMEM((NZ - 1, 4, 2, 128, FEAT), BF),
            pltpu.VMEM((4, 128, FEAT), BF),
            pltpu.VMEM((4, 128, FEAT), BF),
            pltpu.VMEM((ROWS, FEAT), F32),
            pltpu.VMEM((ROWS, FEAT), F32),
            pltpu.VMEM((ROWS, FEAT), BF),
            pltpu.VMEM((RANK, SLOTS), BF),
            pltpu.VMEM((N_TEN - 1, 16, LANES), BF),
            pltpu.VMEM((RANK, SLOTS), BF),
            pltpu.VMEM((RANK, SLOTS), BF),
            pltpu.VMEM((N_TEN - 1, 16, LANES), BF),
            pltpu.VMEM((RANK, SLOTS), BF),
            pltpu.VMEM((1, SLOTS), F32),
            pltpu.VMEM((SLOTS, 128), F32),
            pltpu.VMEM((4, 128, 128), F32),
            pltpu.VMEM((16, 128), F32),
            pltpu.VMEM((N_TEN - 1, 16, 128), F32),
            pltpu.VMEM((N_DP, 8, 128), F32),
            pltpu.VMEM((N_DP, 8, 128), F32),
            dma((6,)),
            dma((NZ,)),
            dma((3, 2, N_DP - 1)),
            dma((len(PHASES), 2, N_DP - 1)),
            dma((2, N_DP - 1)),
            dma((2, len(PHASES), NZ - 1, 4)),
            dma((5, 4, N_TEN - 1)),
            dma((2, len(PHASES), 4)),
            dma((2, N_TEN - 1)),
        ],
        compiler_params=pltpu.CompilerParams(
            collective_id=0, has_side_effects=True, vmem_limit_bytes=58 << 20
        ),
        name="step",
    )(
        tokens,
        proj,
        gain.reshape(1, FEAT),
        target,
        adapter_down_weight.reshape(wide, FEAT),
        adapter_up_weight.reshape(wide, FEAT),
        source_row_index,
        padded_row_index,
        padded_block_tenant,
    )
    draft, grad_down, grad_up = pl.pallas_call(
        hand_on,
        out_shape=results,
        in_specs=[hbm] * 3,
        out_specs=(hbm,) * 3,
        scratch_shapes=[dma((12,))],
        compiler_params=pltpu.CompilerParams(vmem_limit_bytes=8 << 20),
        name="hand_on",
    )(*made)
    return (
        draft,
        grad_down.reshape(TEN, RANK, FEAT),
        grad_up.reshape(TEN, RANK, FEAT),
    )


def solution(mesh):
    return jax.shard_map(
        body,
        mesh=mesh,
        in_specs=(
            P("dp", "tensor"),
            P("tensor", None),
            P("tensor"),
            P("dp", "tensor"),
            P("dp", None, "tensor"),
            P("dp", None, "tensor"),
            P("dp", None, None),
            P("dp", None),
            P("dp", None),
        ),
        out_specs=(P("dp", "tensor"), P("dp", None, "tensor"), P("dp", None, "tensor")),
        check_vma=False,
    )
```

```python
import jax
import jax.numpy as jnp
from jax import lax
from jax.experimental import pallas as pl
from jax.experimental.pallas import tpu as pltpu
from jax.sharding import PartitionSpec as P

MODEL_WIDTH = 8192
MESH = pl.DeviceIdType.MESH
BF = jnp.bfloat16
F32 = jnp.float32
NT = (((1,), (1,)), ((), ()))
TN = (((0,), (0,)), ((), ()))

N_DP = 16
N_TEN = 16
NZ = 8
CAP = 96
SLOTS = N_DP * CAP
TEN = 16
RANK = 64
ROWS = 512
FEAT = 512
LANES = SLOTS // 4
PHASES = ((0, 384), (384, 128))


def aligned(value, multiple):
    return pl.multiple_of(value, multiple)


def kernel(
    tok, proj, gain, target, down, up, routes, positions, blocks,
    draft_out, gdown_out, gup_out,
    draft, gdown, gup, proj_v, onehot, tok_out, tgt_out, delta_out, h_out, feat, tgt_slots,
    back_slots, h_slots, gslots, expand, expand_t,
    part, first, ring, ysend, yrecv, hidden, delta_rows, h_rows,
    rank_part, rank_land, rank_full, back_part, back_land, back_full,
    trow, tcol, stat_acc, stat_send, stat_land, scal_send, scal_land,
    out_sem, proj_sem, a2a_sem, h_sem, scal_sem, ring_sem, ar_sem, y_sem, stat_sem,
):
    dp = lax.axis_index("dp")
    ten = lax.axis_index("tensor")
    z, y = ten // 2, ten % 2

    barrier = pltpu.get_barrier_semaphore()

    def greet(d, carry):
        pl.semaphore_signal(
            barrier, inc=1, device_id=((dp + d) % N_DP, ten), device_id_type=MESH
        )
        pl.semaphore_signal(
            barrier, inc=1, device_id=(dp, (ten + d) % N_TEN), device_id_type=MESH
        )
        return carry

    lax.fori_loop(1, N_DP, greet, 0)

    def chunk_cols(c):
        return pl.ds(aligned(c * 1024, 1024), 1024)

    def load_proj(c):
        return pltpu.make_async_copy(
            proj.at[:, chunk_cols(c)], proj_v.at[:, chunk_cols(c)], proj_sem.at[c]
        )

    for place in (7, 1, 6, 2, 5, 3, 4, 0):
        load_proj((z + place) % NZ).start()

    route = jnp.concatenate(
        [routes[0].astype(F32), jnp.zeros((N_DP, 128 - CAP), F32)], axis=1
    )
    route = jnp.concatenate([route, jnp.zeros((128 - N_DP, 128), F32)], axis=0).T
    row_number = lax.broadcasted_iota(jnp.int32, (CAP, ROWS), 1).astype(F32)
    for d in range(N_DP):
        hit = jnp.broadcast_to(route[0:CAP, d : d + 1], (CAP, ROWS)) == row_number
        onehot[d * CAP : (d + 1) * CAP, :] = jnp.where(hit, 1.0, 0.0).astype(BF)

    def to_slots(src, dst, cols=pl.ds(0, FEAT)):
        def one(b, carry):
            rows = pl.ds(aligned(b * 384, 384), 384)
            dst[rows, cols] = jnp.dot(
                onehot[rows, :], src[:, cols], preferred_element_type=F32
            ).astype(BF)
            return carry

        lax.fori_loop(0, 4, one, 0)

    def slot_rows(s):
        return pl.ds(aligned(s * CAP, 32), CAP)

    everything = pl.ds(0, FEAT)

    def a2a_copy(src, dst, sems, cols, d):
        peer = (dp + d) % N_DP
        return pltpu.make_async_remote_copy(
            src_ref=src.at[slot_rows(peer), cols],
            dst_ref=dst.at[slot_rows(dp), cols],
            send_sem=sems.at[0, d - 1],
            recv_sem=sems.at[1, d - 1],
            device_id=(peer, ten),
            device_id_type=MESH,
        )

    def each_peer(action):
        def one(k, carry):
            action(N_TEN // 2 + (1 - 2 * (k % 2)) * ((k + 1) // 2))
            return carry

        lax.fori_loop(0, N_TEN - 1, one, 0)

    def a2a_start(src, dst, sems, cols=everything):
        each_peer(lambda d: a2a_copy(src, dst, sems, cols, d).start())
        dst[slot_rows(dp), cols] = src[slot_rows(dp), cols]

    def a2a_wait(src, dst, sems, cols=everything):
        each_peer(lambda d: a2a_copy(src, dst, sems, cols, d).wait())

    def stream_rows(i):
        return pl.ds(aligned(i * 128, 128), 128)

    def sign(i):
        return 1 - 2 * (i // 2)

    def part_cols(p):
        return pl.ds(*PHASES[p])

    def ring_copy(p, s, i):
        here = first.at[i] if s == 0 else ring.at[s - 1, i]
        peer = ((z + sign(i) + NZ) % NZ) * 2 + y
        return pltpu.make_async_remote_copy(
            src_ref=here.at[:, :, part_cols(p)],
            dst_ref=ring.at[s, i, :, :, part_cols(p)],
            send_sem=ring_sem.at[0, p, s, i],
            recv_sem=ring_sem.at[1, p, s, i],
            device_id=(dp, peer),
            device_id_type=MESH,
        )

    def partials(p, s):
        if p == 0 and s == 0:
            load_proj((z + 7) % NZ).wait()
            load_proj((z + 1) % NZ).wait()
        elif p == 0 and s < 3:
            load_proj((z + 7 - s) % NZ).wait()
            load_proj((z + 1 + s) % NZ).wait()
        elif p == 0 and s == 3:
            load_proj((z + 4) % NZ).wait()
        elif p == 0 and s == 7:
            load_proj(z).wait()
        start, width = PHASES[p]

        def one(way, carry):
            c = (z + 2 * NZ - (1 - 2 * way) * (s + 1)) % NZ
            rows = pl.ds(aligned(way * 256, 256), 256)
            for j in range(2):
                cols = pl.ds(aligned(c * 1024 + j * 512 + start, 128), width)
                part[way, j, :, part_cols(p)] = jnp.dot(
                    tok[rows, :], proj_v[:, cols], preferred_element_type=F32
                )
            return carry

        lax.fori_loop(0, 2, one, 0)

    def my_part(p, i, j):
        rows = pl.ds(aligned((i % 2) * 128, 128), 128)
        return part[i // 2, j, rows, part_cols(p)]

    def each_stream(action):
        def one(k, carry):
            action((k % 2) * 2 + k // 2)
            return carry

        lax.fori_loop(0, 4, one, 0)

    def first_sends(p):
        def one(i):
            for j in range(2):
                first[i, j, :, part_cols(p)] = my_part(p, i, j).astype(BF)
            ring_copy(p, 0, i).start()

        each_stream(one)
        partials(p, 1)

    def ring_step(p, s):
        def one(i):
            ring_copy(p, s - 1, i).wait_recv()
            for j in range(2):
                ring[s - 1, i, j, :, part_cols(p)] = (
                    my_part(p, i, j) + ring[s - 1, i, j, :, part_cols(p)].astype(F32)
                ).astype(BF)
            ring_copy(p, s, i).start()

        each_stream(one)
        partials(p, s + 1)

    def y_copy(p, i):
        return pltpu.make_async_remote_copy(
            src_ref=ysend.at[i, :, part_cols(p)],
            dst_ref=yrecv.at[i, :, part_cols(p)],
            send_sem=y_sem.at[0, p, i],
            recv_sem=y_sem.at[1, p, i],
            device_id=(dp, z * 2 + 1 - y),
            device_id_type=MESH,
        )

    def last_hop(p):
        cols = part_cols(p)

        def one(i):
            ring_copy(p, NZ - 2, i).wait_recv()
            ysend[i, :, cols] = (
                my_part(p, i, 1 - y) + ring[NZ - 2, i, 1 - y, :, cols].astype(F32)
            ).astype(BF)
            y_copy(p, i).start()
            hidden[stream_rows(i), cols] = my_part(p, i, y) + ring[
                NZ - 2, i, y, :, cols
            ].astype(F32)

        each_stream(one)

    def y_finish(p):
        cols = part_cols(p)

        def one(i, carry):
            y_copy(p, i).wait()
            rows = stream_rows(i)
            total = hidden[rows, cols] + yrecv[i, :, cols].astype(F32)
            hidden[rows, cols] = total
            h_rows[rows, cols] = total.astype(BF)
            return carry

        lax.fori_loop(0, 4, one, 0)

    def to_owners(p):
        to_slots(h_rows, h_out, part_cols(p))
        a2a_start(h_out, h_slots, h_sem.at[p], part_cols(p))

    def chunk(arr, t, g, n):
        wide = LANES // n
        return arr.at[
            pl.ds(aligned((t // 4) * 16, 16), 16),
            pl.ds(aligned(g * 4 * wide + (t % 4) * wide, 128), wide),
        ]

    def landed(land, d, g, n):
        return land.at[d, :, pl.ds(g * (LANES // n), LANES // n)]

    def scatter_copy(part, land, g, n, d):
        peer = (ten + d) % N_TEN
        return pltpu.make_async_remote_copy(
            src_ref=chunk(part, peer, g, n),
            dst_ref=landed(land, d - 1, g, n),
            send_sem=ar_sem.at[n - 1 + g, 0, d - 1],
            recv_sem=ar_sem.at[n - 1 + g, 1, d - 1],
            device_id=(dp, peer),
            device_id_type=MESH,
        )

    def spread_copy(full, g, n, d):
        return pltpu.make_async_remote_copy(
            src_ref=chunk(full, ten, g, n),
            dst_ref=chunk(full, ten, g, n),
            send_sem=ar_sem.at[n - 1 + g, 2, d - 1],
            recv_sem=ar_sem.at[n - 1 + g, 3, d - 1],
            device_id=(dp, (ten + d) % N_TEN),
            device_id_type=MESH,
        )

    def ar_first(part, land, g, n):
        each_peer(lambda d: scatter_copy(part, land, g, n, d).start())

    def ar_second(part, land, full, g, n):
        each_peer(lambda d: scatter_copy(part, land, g, n, d).wait())
        total = chunk(part, ten, g, n)[...].astype(F32)
        for d in range(N_TEN - 1):
            total = total + landed(land, d, g, n)[...].astype(F32)
        chunk(full, ten, g, n)[...] = total.astype(BF)
        each_peer(lambda d: spread_copy(full, g, n, d).start())

    def ar_wait(full, g, n):
        each_peer(lambda d: spread_copy(full, g, n, d).wait())

    def low_rank(weights, rows_ref, scale, out, tiles=(0, SLOTS // 256)):
        def one(j, carry):
            lanes = pl.ds(aligned(j * 256, 256), 256)
            full = lax.dot_general(
                weights[...], rows_ref[lanes, :], NT, preferred_element_type=F32
            )
            tenant = jnp.broadcast_to(trow[:, lanes], (RANK, 256))
            total = jnp.zeros((RANK, 256), F32)
            for t in range(TEN):
                total = total + jnp.where(
                    tenant == t + 1.0, full[t * RANK : (t + 1) * RANK, :], 0.0
                )
            out[:, lanes] = (scale * total).astype(BF)
            return carry

        lax.fori_loop(*tiles, one, 0)

    def spread_tenants(full, tiles=(0, SLOTS // 256)):
        def one(j, carry):
            lanes = pl.ds(aligned(j * 256, 256), 256)
            value = full[:, lanes].astype(F32)
            tenant = jnp.broadcast_to(trow[:, lanes], (RANK, 256))
            for t in range(TEN):
                expand_t[t * RANK : (t + 1) * RANK, lanes] = jnp.where(
                    tenant == t + 1.0, value, 0.0
                ).astype(BF)
            return carry

        lax.fori_loop(*tiles, one, 0)

    def grouped_outer(rows_ref, scale, out, after=None):
        def one(t, carry):
            rows = pl.ds(aligned(t * 256, 256), 256)
            out[rows, :] = (
                scale
                * jnp.dot(expand_t[rows, :], rows_ref[...], preferred_element_type=F32)
            ).astype(BF)
            if after:
                after(t).start()
            return carry

        lax.fori_loop(0, TEN * RANK // 256, one, 0)

    def slot_tenants():
        held = positions[...]
        count = held.shape[1]
        owner = jnp.concatenate(
            [
                jnp.broadcast_to(blocks[:, b : b + 1].astype(F32) + 1.0, (1, 128))
                for b in range(count // 128)
            ],
            axis=1,
        )
        high = jnp.where(
            jnp.broadcast_to(held // 128, (16, count))
            == lax.broadcasted_iota(jnp.int32, (16, count), 0),
            1.0,
            0.0,
        ).astype(BF)
        low = jnp.where(
            jnp.broadcast_to(held % 128, (128, count))
            == lax.broadcasted_iota(jnp.int32, (128, count), 0),
            jnp.broadcast_to(owner, (128, count)),
            0.0,
        ).astype(BF)
        table = lax.dot_general(high, low, NT, preferred_element_type=F32)
        columns = jnp.concatenate([table, jnp.zeros((112, 128), F32)], axis=0).T
        for a in range(SLOTS // 128):
            trow[:, a * 128 : (a + 1) * 128] = table[a : a + 1, :]
            tcol[a * 128 : (a + 1) * 128, :] = jnp.broadcast_to(
                columns[:, a : a + 1], (128, 128)
            )

    def deltas(b, carry):
        rows = pl.ds(aligned(b * 256, 256), 256)
        value = rank_full[:, rows].astype(F32)
        twice = jnp.concatenate([value, value], axis=0).T
        lane = lax.broadcasted_iota(jnp.int32, (256, 128), 1)
        tenant = tcol[rows, :] - jnp.where(lane >= RANK, 1.0, 0.0)
        for j in range(TEN // 2):
            expand[:, j * 128 : (j + 1) * 128] = jnp.where(
                tenant == 2.0 * j + 1.0, twice, 0.0
            ).astype(BF)
        delta_out[rows, :] = (
            2.0 * jnp.dot(expand[...], up[...], preferred_element_type=F32)
        ).astype(BF)
        return carry

    def scatter_rows():
        for q in range(4):
            cols = pl.ds(q * 128, 128)
            delta_rows[cols, :] = lax.dot_general(
                onehot[:, cols], back_slots[...], TN, preferred_element_type=F32
            )

    def stats(p, i):
        rows, cols = pl.ds(i * 128, 128), part_cols(p)
        h = hidden[rows, cols] + delta_rows[rows, cols]
        hidden[rows, cols] = h
        gh = gain[:, cols] * h
        s1 = jnp.sum(h * h, axis=1, keepdims=True)
        s2 = jnp.sum(gh * gh, axis=1, keepdims=True)
        s3 = jnp.sum(gh * target[rows, cols].astype(F32), axis=1, keepdims=True)
        lane = lax.broadcasted_iota(jnp.int32, (128, 128), 1)
        return jnp.where(lane == 0, s1, jnp.where(lane == 1, s2, s3))

    def early_stats():
        for i in range(4):
            stat_acc[i] = stats(0, i)

    to_slots(tok, tok_out)
    partials(0, 0)
    pl.semaphore_wait(barrier, 2 * (N_DP - 1))
    a2a_start(tok_out, feat, a2a_sem.at[0])
    first_sends(0)
    scal_send[...] = jnp.zeros_like(scal_send)
    slot_tenants()
    to_slots(target, tgt_out)
    a2a_start(tgt_out, tgt_slots, a2a_sem.at[2])
    ring_step(0, 1)
    ring_step(0, 2)
    a2a_wait(tok_out, feat, a2a_sem.at[0])
    low_rank(down, feat, 1.0, rank_part)
    ar_first(rank_part, rank_land, 0, 1)
    ring_step(0, 3)
    ar_second(rank_part, rank_land, rank_full, 0, 1)
    ring_step(0, 4)
    ar_wait(rank_full, 0, 1)
    lax.fori_loop(0, SLOTS // 256, deltas, 0)
    a2a_start(delta_out, back_slots, a2a_sem.at[1])
    ring_step(0, 5)
    partials(1, 0)
    first_sends(1)
    ring_step(0, 6)
    ring_step(1, 1)
    last_hop(0)
    ring_step(1, 2)
    ring_step(1, 3)
    y_finish(0)
    to_owners(0)
    ring_step(1, 4)
    ring_step(1, 5)
    a2a_wait(delta_out, back_slots, a2a_sem.at[1])
    scatter_rows()
    early_stats()
    ring_step(1, 6)
    spread_tenants(rank_full)
    last_hop(1)
    y_finish(1)

    for i in range(4):
        table = stat_acc[i] + stats(1, i)
        stat_send[4 * i : 4 * i + 4, :] = table.T[0:4, :]

    def stat_copy(d):
        return pltpu.make_async_remote_copy(
            src_ref=stat_send,
            dst_ref=stat_land.at[d - 1],
            send_sem=stat_sem.at[0, d - 1],
            recv_sem=stat_sem.at[1, d - 1],
            device_id=(dp, (ten + d) % N_TEN),
            device_id_type=MESH,
        )

    each_peer(lambda d: stat_copy(d).start())
    to_owners(1)
    each_peer(lambda d: stat_copy(d).wait())

    total = stat_send[...]
    for d in range(N_TEN - 1):
        total = total + stat_land[d]
    invs, dots = [], []
    for i in range(4):
        s1, s2, s3 = (total[4 * i + q : 4 * i + q + 1, :] for q in range(3))
        inv = lax.rsqrt(s1 / MODEL_WIDTH + 1e-05)
        invs.append(inv)
        dots.append(inv * (inv * s2 - s3) / (8.0 * MODEL_WIDTH))

    pieces = []
    for rest in (jnp.concatenate(invs, axis=1), jnp.concatenate(dots, axis=1)):
        for _ in range(3):
            piece = rest.astype(BF).astype(F32)
            pieces.append(piece)
            rest = rest - piece
    pieces.append(jnp.zeros((10, ROWS), F32))
    placed = lax.dot_general(
        jnp.concatenate(pieces, axis=0).astype(BF),
        onehot[...],
        NT,
        preferred_element_type=F32,
    )
    pair = jnp.concatenate(
        [
            placed[0:1] + placed[1:2] + placed[2:3],
            placed[3:4] + placed[4:5] + placed[5:6],
        ],
        axis=0,
    )
    for d in range(N_DP):
        scal_send[d, 0:2, 0:CAP] = pair[:, d * CAP : (d + 1) * CAP]

    def scal_copy(d):
        peer = (dp + d) % N_DP
        return pltpu.make_async_remote_copy(
            src_ref=scal_send.at[peer],
            dst_ref=scal_land.at[dp],
            send_sem=scal_sem.at[0, d - 1],
            recv_sem=scal_sem.at[1, d - 1],
            device_id=(peer, ten),
            device_id_type=MESH,
        )

    each_peer(lambda d: scal_copy(d).start())
    scal_land[dp] = scal_send[dp]

    for i in range(4):
        rows = pl.ds(i * 128, 128)
        table = jnp.concatenate([invs[i], jnp.zeros((127, 128), F32)], axis=0).T
        inv = table[:, 0:1]
        draft[rows, :] = (hidden[rows, :] * inv * gain[...]).astype(BF)
    store_draft = pltpu.make_async_copy(draft, draft_out, out_sem.at[0])
    store_draft.start()

    a2a_wait(tgt_out, tgt_slots, a2a_sem.at[2])
    for p in range(len(PHASES)):
        a2a_wait(h_out, h_slots, h_sem.at[p], part_cols(p))
    each_peer(lambda d: scal_copy(d).wait())

    def grads(s, carry):
        rows = slot_rows(s)
        table = jnp.concatenate([scal_land[s], jnp.zeros((120, 128), F32)], axis=0).T
        inv, dot = table[0:CAP, 0:1], table[0:CAP, 1:2]
        g = gain[...]
        h = h_slots[rows, :].astype(F32) + delta_out[rows, :].astype(F32)
        scaled = h * inv
        weighted = g * ((scaled * g - tgt_slots[rows, :].astype(F32)) / 8.0)
        gslots[rows, :] = (inv * (weighted - scaled * dot)).astype(BF)
        return carry

    for g, sources in enumerate(((0, 6), (6, 11), (11, N_DP))):
        lax.fori_loop(*sources, grads, 0)
        low_rank(up, gslots, 2.0, back_part, (2 * g, 2 * g + 2))
        ar_first(back_part, back_land, g, 3)
    for g in range(3):
        ar_second(back_part, back_land, back_full, g, 3)
    grouped_outer(gslots, 2.0, gup)
    store_up = pltpu.make_async_copy(gup, gup_out, out_sem.at[1])
    store_up.start()
    for g in range(3):
        ar_wait(back_full, g, 3)
        spread_tenants(back_full, (2 * g, 2 * g + 2))

    def store_down(t):
        rows = pl.ds(aligned(t * 256, 256), 256)
        return pltpu.make_async_copy(
            gdown.at[rows, :], gdown_out.at[rows, :], out_sem.at[2 + t]
        )

    grouped_outer(feat, 1.0, gdown, store_down)

    for p in range(len(PHASES)):
        for s in range(NZ - 1):

            def drain(i, carry, p=p, s=s):
                ring_copy(p, s, i).wait_send()
                return carry

            lax.fori_loop(0, 4, drain, 0)

    store_draft.wait()
    store_up.wait()
    for t in range(4):
        store_down(t).wait()


def hand_on(*refs):
    sems = refs[-1]
    copies = []
    for k in range(3):
        src, dst = refs[k], refs[3 + k]
        size = src.shape[0] // 4
        for q in range(4):
            rows = pl.ds(q * size, size)
            copies.append(
                pltpu.make_async_copy(
                    src.at[rows, :], dst.at[rows, :], sems.at[4 * k + q]
                )
            )
    for copy in copies:
        copy.start()
    for copy in copies:
        copy.wait()


def body(
    tokens,
    proj,
    gain,
    target,
    adapter_down_weight,
    adapter_up_weight,
    source_row_index,
    padded_row_index,
    padded_block_tenant,
):
    vmem = pl.BlockSpec(memory_space=pltpu.VMEM)
    hbm = pl.BlockSpec(memory_space=pl.ANY)
    wide = TEN * RANK
    dma = pltpu.SemaphoreType.DMA
    results = (
        jax.ShapeDtypeStruct((ROWS, FEAT), BF),
        jax.ShapeDtypeStruct((wide, FEAT), BF),
        jax.ShapeDtypeStruct((wide, FEAT), BF),
    )
    made = pl.pallas_call(
        kernel,
        out_shape=results,
        in_specs=[vmem, hbm] + [vmem] * 7,
        out_specs=(hbm, hbm, hbm),
        scratch_shapes=[
            pltpu.VMEM((ROWS, FEAT), BF),
            pltpu.VMEM((wide, FEAT), BF),
            pltpu.VMEM((wide, FEAT), BF),
            pltpu.VMEM((FEAT, MODEL_WIDTH), BF),
            pltpu.VMEM((SLOTS, ROWS), BF),
            pltpu.VMEM((SLOTS, FEAT), BF),
            pltpu.VMEM((SLOTS, FEAT), BF),
            pltpu.VMEM((SLOTS, FEAT), BF),
            pltpu.VMEM((SLOTS, FEAT), BF),
            pltpu.VMEM((SLOTS, FEAT), BF),
            pltpu.VMEM((SLOTS, FEAT), BF),
            pltpu.VMEM((SLOTS, FEAT), BF),
            pltpu.VMEM((SLOTS, FEAT), BF),
            pltpu.VMEM((SLOTS, FEAT), BF),
            pltpu.VMEM((256, wide), BF),
            pltpu.VMEM((wide, SLOTS), BF),
            pltpu.VMEM((2, 2, 256, FEAT), F32),
            pltpu.VMEM((4, 2, 128, FEAT), BF),
            pltpu.VMEM((NZ - 1, 4, 2, 128, FEAT), BF),
            pltpu.VMEM((4, 128, FEAT), BF),
            pltpu.VMEM((4, 128, FEAT), BF),
            pltpu.VMEM((ROWS, FEAT), F32),
            pltpu.VMEM((ROWS, FEAT), F32),
            pltpu.VMEM((ROWS, FEAT), BF),
            pltpu.VMEM((RANK, SLOTS), BF),
            pltpu.VMEM((N_TEN - 1, 16, LANES), BF),
            pltpu.VMEM((RANK, SLOTS), BF),
            pltpu.VMEM((RANK, SLOTS), BF),
            pltpu.VMEM((N_TEN - 1, 16, LANES), BF),
            pltpu.VMEM((RANK, SLOTS), BF),
            pltpu.VMEM((1, SLOTS), F32),
            pltpu.VMEM((SLOTS, 128), F32),
            pltpu.VMEM((4, 128, 128), F32),
            pltpu.VMEM((16, 128), F32),
            pltpu.VMEM((N_TEN - 1, 16, 128), F32),
            pltpu.VMEM((N_DP, 8, 128), F32),
            pltpu.VMEM((N_DP, 8, 128), F32),
            dma((6,)),
            dma((NZ,)),
            dma((3, 2, N_DP - 1)),
            dma((len(PHASES), 2, N_DP - 1)),
            dma((2, N_DP - 1)),
            dma((2, len(PHASES), NZ - 1, 4)),
            dma((5, 4, N_TEN - 1)),
            dma((2, len(PHASES), 4)),
            dma((2, N_TEN - 1)),
        ],
        compiler_params=pltpu.CompilerParams(
            collective_id=0, has_side_effects=True, vmem_limit_bytes=58 << 20
        ),
        name="step",
    )(
        tokens,
        proj,
        gain.reshape(1, FEAT),
        target,
        adapter_down_weight.reshape(wide, FEAT),
        adapter_up_weight.reshape(wide, FEAT),
        source_row_index,
        padded_row_index,
        padded_block_tenant,
    )
    draft, grad_down, grad_up = pl.pallas_call(
        hand_on,
        out_shape=results,
        in_specs=[hbm] * 3,
        out_specs=(hbm,) * 3,
        scratch_shapes=[dma((12,))],
        compiler_params=pltpu.CompilerParams(vmem_limit_bytes=8 << 20),
        name="hand_on",
    )(*made)
    return (
        draft,
        grad_down.reshape(TEN, RANK, FEAT),
        grad_up.reshape(TEN, RANK, FEAT),
    )


def solution(mesh):
    return jax.shard_map(
        body,
        mesh=mesh,
        in_specs=(
            P("dp", "tensor"),
            P("tensor", None),
            P("tensor"),
            P("dp", "tensor"),
            P("dp", None, "tensor"),
            P("dp", None, "tensor"),
            P("dp", None, None),
            P("dp", None),
            P("dp", None),
        ),
        out_specs=(P("dp", "tensor"), P("dp", None, "tensor"), P("dp", None, "tensor")),
        check_vma=False,
    )
```
